32 devices in a mesh: grp: 2 (over core), ctx: 8 (over z, x), hd: 2 (over y).
Axes of the slice: x: 2, y: 2, z: 4, core: 2. Of those that a mesh axis runs over, the one named last changes fastest.
Arguments:
- video_q: bfloat16 [1024, 24, 128], P(('ctx', 'hd'), 'grp'), may hold values from -6 to 6
- video_k: bfloat16 [1024, 24, 128], P(('ctx', 'hd'), 'grp'), may hold values from -6 to 6
- video_v: bfloat16 [1024, 24, 128], P(('ctx', 'hd'), 'grp'), may hold values from -6 to 6
- positions: int32 [3, 1024], P(None, ('ctx', 'hd')), may hold values from 0 to 15, as said below
- text_q: bfloat16 [256, 24, 128], P(None, ('grp', 'hd')), may hold values from -16 to 16
- text_k: bfloat16 [256, 24, 128], P(None, ('grp', 'hd')), may hold values from -16 to 16
- text_v: bfloat16 [256, 24, 128], P(None, ('grp', 'hd')), may hold values from -6 to 6
- text_count: int32 [1], replicated, may hold values from 64 to 256
Outputs:
- video_out: bfloat16 [1024, 24, 128], P(('ctx', 'hd'), 'grp')
- text_out: bfloat16 [256, 24, 128], P('ctx', ('grp', 'hd'))
The draws below stay inside these ranges and needn't reach their ends.
Inputs may be any that keep to these rules, and one draw needn't show every extreme that they name: `positions`: column n holds the frame, row and column of video token n; the columns are distinct cells of a grid of 4 frames of 16 by 16 cells.
All inputs are finite; a program needn't handle non-finite values.
Results may differ from the reference program's by a relative error of at most 0.0073.
Values may be sent and summed in bfloat16 or wider, within the bound.
A program may use at most 128 MiB of HBM per device.

```python
import math
import jax
import jax.numpy as jnp
from jax import lax

HEADS = 24
HD = 128
TXT = 256
GRID_H = 16
GRID_W = 16
TOKENS = 1024


def text_pair(key):
    array_shape = (TXT, HEADS, HD)
    keys_base = jnp.clip(jax.random.normal(jax.random.fold_in(key, 101), array_shape, jnp.float32), -3.2, 3.2)
    query_base = jnp.clip(jax.random.normal(jax.random.fold_in(key, 102), array_shape, jnp.float32), -3.2, 3.2)
    return (query_base, keys_base)


def draw_text_q(key, part):
    return text_pair(key)[0].astype(jnp.bfloat16)


def draw_text_k(key, part):
    return text_pair(key)[1].astype(jnp.bfloat16)


def draw_positions(key, part):
    ordering = jax.random.permutation(jax.random.fold_in(key, 7), TOKENS)
    cell_count = GRID_H * GRID_W
    frame_at = ordering // cell_count
    row_at = ordering // GRID_W % GRID_H
    column = ordering % GRID_W
    return jnp.stack([frame_at, row_at, column]).astype(jnp.int32)


def steps_of(stream_key, extent, shards, least, high):
    level = 1.0
    for axis_at, shards_of in shards:
        heights = jax.random.uniform(jax.random.fold_in(jax.random.fold_in(stream_key, 6), axis_at), (shards_of,), jnp.float32, least / len(shards), high / len(shards))
        level = level * jnp.repeat(jnp.exp(heights), extent[axis_at] // shards_of).reshape((-1,) + (1,) * (len(extent) - 1 - axis_at))
    return level


def gaussian(own_key, extent, deviation, bound, cuts=(), held_as=jnp.bfloat16):
    loudness = steps_of(own_key, extent, cuts, -0.22, 0.18) if cuts else 1.0
    entries = jax.random.normal(own_key, extent, jnp.float32) * deviation * loudness
    return jnp.minimum(jnp.maximum(entries, -bound), bound).astype(held_as)


def setup_inputs(seed: int = 0) -> dict:
    arg_keys = jax.random.split(jax.random.key(seed), 9)
    return {
        "video_q": gaussian(arg_keys[0], (TOKENS, HEADS, HD), 1.0, 6.0, ((0, 16), (1, 2))),
        "video_k": gaussian(arg_keys[1], (TOKENS, HEADS, HD), 1.0, 6.0, ((0, 16), (1, 2))),
        "video_v": gaussian(arg_keys[2], (TOKENS, HEADS, HD), 1.0, 6.0, ((0, 16), (1, 2))),
        "positions": draw_positions(jax.random.fold_in(arg_keys[8], 71), 0),
        "text_q": draw_text_q(jax.random.fold_in(arg_keys[8], 71), 0),
        "text_k": draw_text_k(jax.random.fold_in(arg_keys[8], 71), 0),
        "text_v": gaussian(arg_keys[6], (TXT, HEADS, HD), 1.0, 6.0, ((1, 4),)),
        "text_count": jax.random.randint(arg_keys[7], (1,), TXT // 4, TXT + 1).astype(jnp.int32),
    }


THETA = 256.0

def rotate(tokens_in, positions):
    head_dim = tokens_in.shape[-1]
    band_t = head_dim // 8
    band_h = (head_dim - band_t) // 2
    band_w = head_dim - band_t - band_h
    values = tokens_in.astype(jnp.float32)
    pieces = []
    offset = 0
    for axis_index, band_size in ((0, band_t), (1, band_h), (2, band_w)):
        half_size = band_size // 2
        frequency = THETA ** (-2.0 * jnp.arange(half_size, dtype=jnp.float32) / band_size)
        angles = positions[axis_index].astype(jnp.float32)[:, None] * frequency[None, :]
        cos_table = jnp.cos(angles)[:, None, :]
        sin_table = jnp.sin(angles)[:, None, :]
        lower_half = values[:, :, offset:offset + half_size]
        upper_half = values[:, :, offset + half_size:offset + band_size]
        pieces.append(lower_half * cos_table - upper_half * sin_table)
        pieces.append(upper_half * cos_table + lower_half * sin_table)
        offset += band_size
    return jnp.concatenate(pieces, axis=-1).astype(jnp.bfloat16)

def reference(video_q, video_k, video_v, positions, text_q, text_k, text_v, text_count):
    rot_q = rotate(video_q, positions)
    rot_k = rotate(video_k, positions)
    queries = jnp.moveaxis(jnp.concatenate([rot_q, text_q], axis=0), 1, 0)
    keys_all = jnp.moveaxis(jnp.concatenate([rot_k, text_k], axis=0), 1, 0)
    values_all = jnp.moveaxis(jnp.concatenate([video_v, text_v], axis=0), 1, 0)
    live = jnp.concatenate([jnp.ones((TOKENS,), dtype=bool), jnp.arange(TXT, dtype=jnp.int32) < text_count[0]])
    scale = 1.0 / math.sqrt(HD)

    def head_attention(operands):
        q_head, k_head, v_head = operands
        scores = jnp.dot(q_head, k_head.T, preferred_element_type=jnp.float32) * scale
        scores = jnp.where(live[None, :], scores, -jnp.inf)
        peak = lax.optimization_barrier(jnp.max(scores, axis=1, keepdims=True))
        probs = jnp.exp(scores - peak)
        total = lax.optimization_barrier(jnp.sum(probs, axis=1, keepdims=True))
        mixed = jnp.dot(probs.astype(jnp.bfloat16), v_head, preferred_element_type=jnp.float32)
        return (mixed / total).astype(jnp.bfloat16)
    attended = jnp.moveaxis(lax.map(head_attention, (queries, keys_all, values_all)), 0, 1)
    video_out = attended[:TOKENS]
    text_out = attended[TOKENS:]
    return (video_out, text_out)
```

```python
import functools
import math

import jax
import jax.numpy as jnp
import numpy as np
from jax import lax
from jax.experimental import pallas as pl
from jax.experimental.pallas import tpu as pltpu
from jax.sharding import PartitionSpec as P

THETA = 256.0
MESH = pl.DeviceIdType.MESH
PAIR = 2
NEAR = 2


def bands(dim):
    band_t = dim // 8
    band_h = (dim - band_t) // 2
    return (band_t, band_h, dim - band_t - band_h)


def constants(dim):
    axis = np.zeros((dim,), np.int32)
    freq = np.zeros((dim,), np.float32)
    swap = np.zeros((dim, dim), np.float32)
    start = 0
    for index, size in enumerate(bands(dim)):
        half = size // 2
        for i in range(half):
            low, high = start + i, start + half + i
            axis[low] = axis[high] = index
            freq[low] = freq[high] = np.float32(THETA ** (-2.0 * i / size))
            swap[high, low] = -1.0
            swap[low, high] = 1.0
        start += size
    return axis, freq, swap


def each(count, body):
    if count <= 4:
        for i in range(count):
            body(i)
    else:
        lax.fori_loop(0, count, lambda i, _: (body(i), 0)[1], 0)


def kernel(far, hds, q_ref, k_ref, v_ref, cos_ref, sin_ref, swap_ref, tq_ref, tk_ref, tv_ref, count_ref,
           out_ref, tout_ref, qs, ks, qg, kv, ost, tst, acc, peak, total,
           a_send, q_recv, kv_recv, f_send, n_send, o_send, o_recv, t_sems):
    ctx = lax.axis_index("ctx")
    hd = lax.axis_index("hd")
    fi, mi, ni = ctx // (PAIR * NEAR), (ctx // NEAR) % PAIR, ctx % NEAR
    groups = PAIR * hds
    heads = v_ref.shape[1]
    tokens, dim = v_ref.shape[2], v_ref.shape[3]
    mine = hd * PAIR + mi
    slot = fi * NEAR + ni

    def at(f, m, n, h):
        return {"ctx": (f * PAIR + m) * NEAR + n, "hd": h}

    def group_peer(d):
        g = lax.rem(mine + d, groups)
        return g, at(fi, g % PAIR, ni, g // PAIR)

    def far_peer(d):
        f = lax.rem(fi + d, far)
        return f, at(f, mi, ni, hd)

    def near_peer(d):
        n = lax.rem(ni + d, NEAR)
        return n, at(fi, mi, n, hd)

    barrier = pltpu.get_barrier_semaphore()

    def greet(peer):
        pl.semaphore_signal(barrier, inc=1, device_id=peer, device_id_type=MESH)

    each(groups - 1, lambda i: greet(group_peer(i + 1)[1]))
    each(far - 1, lambda i: greet(far_peer(i + 1)[1]))
    each(NEAR - 1, lambda i: greet(near_peer(i + 1)[1]))

    cos, sin, swap = cos_ref[...], sin_ref[...], swap_ref[...]

    def rotate(src, dst):
        for g in range(groups):
            for h in range(heads):
                x = src[g, h]
                turned = jnp.dot(x, swap, preferred_element_type=jnp.float32)
                dst[g, h] = (x.astype(jnp.float32) * cos + turned * sin).astype(jnp.bfloat16)

    rotate(k_ref, ks)
    rotate(q_ref, qs)
    kv[slot, 0, mine] = ks[mine]
    kv[slot, 1, mine] = v_ref[mine]
    qg[mine] = qs[mine]
    pl.semaphore_wait(barrier, (groups - 1) + (far - 1) + (NEAR - 1))

    def remote(src, dst, send, recv, peer):
        return pltpu.make_async_remote_copy(src_ref=src, dst_ref=dst, send_sem=send, recv_sem=recv,
                                            device_id=peer, device_id_type=MESH)

    def kv_to_group(w, d):
        g, peer = group_peer(d)
        src = ks if w == 0 else v_ref
        return remote(src.at[g], kv.at[slot, w, mine], a_send.at[w, d], kv_recv.at[slot, w, mine], peer)

    def q_to_group(d):
        g, peer = group_peer(d)
        return remote(qs.at[g], qg.at[mine], a_send.at[2, d], q_recv.at[mine], peer)

    def kv_to_far(w, g, d):
        f, peer = far_peer(d)
        piece = kv.at[slot, w, g]
        return remote(piece, piece, f_send.at[d, w, g], kv_recv.at[slot, w, g], peer)

    def kv_to_near(s, w, g, d):
        n, peer = near_peer(d)
        piece = kv.at[s, w, g]
        return remote(piece, piece, n_send.at[s // NEAR, w, g], kv_recv.at[s, w, g], peer)

    def arrived(s, w, g):
        piece = kv.at[s, w, g]
        remote(piece, piece, n_send.at[0, w, g], kv_recv.at[s, w, g], near_peer(1)[1]).wait_recv()

    def spread(w, g):
        each(far - 1, lambda i: kv_to_far(w, g, i + 1).start())
        kv_to_near(slot, w, g, 1).start()

    for w in range(2):
        for d in range(1, groups):
            kv_to_group(w, d).start()
        spread(w, mine)
        if w == 0:
            for d in range(1, groups):
                q_to_group(d).start()
    for w in range(2):
        for d in range(1, groups):
            g = lax.rem(mine + d, groups)
            arrived(slot, w, g)
            spread(w, g)

    scale = math.log2(math.e) / math.sqrt(dim)
    rows = groups * tokens

    def queries(h):
        return jnp.concatenate([qg[:, h].reshape(rows, dim), tq_ref[h]], axis=0)

    def score(h, keys):
        return lax.dot_general(queries(h), keys, (((1,), (1,)), ((), ())), preferred_element_type=jnp.float32) * scale

    for d in range(1, groups):
        g = lax.rem(mine + d, groups)
        remote(qg.at[g], qg.at[g], a_send.at[2, d], q_recv.at[g], group_peer(d)[1]).wait_recv()

    for h in range(heads):
        s = score(h, tk_ref[h])
        live = lax.broadcasted_iota(jnp.int32, s.shape, 1) < count_ref[0]
        s = jnp.where(live, s, -jnp.inf)
        top = jnp.max(s, axis=1, keepdims=True)
        p = jnp.exp2(s - top)
        peak[h] = top
        total[h] = jnp.sum(p, axis=1, keepdims=True)
        acc[h] = jnp.dot(p.astype(jnp.bfloat16), tv_ref[h], preferred_element_type=jnp.float32)

    def absorb(h, s):
        keys = kv[s, 0, :, h].reshape(rows, dim)
        values = kv[s, 1, :, h].reshape(rows, dim)
        sc = score(h, keys)
        old = peak[h]
        top = jnp.maximum(old, jnp.max(sc, axis=1, keepdims=True))
        p = jnp.exp2(sc - top)
        factor = jnp.exp2(old - top)
        peak[h] = top
        total[h] = total[h] * factor + jnp.sum(p, axis=1, keepdims=True)
        acc[h] = acc[h] * factor + jnp.dot(p.astype(jnp.bfloat16), values, preferred_element_type=jnp.float32)

    for h in range(heads):
        absorb(h, slot)

    def relay(i):
        s = far_peer(i + 1)[0] * NEAR + ni
        for w in range(2):
            for d in range(groups):
                g = lax.rem(mine + d, groups)
                arrived(s, w, g)
                kv_to_near(s, w, g, 1).start()
    each(far - 1, relay)

    other = near_peer(1)[0]

    def take(s):
        for w in range(2):
            for d in range(groups):
                arrived(s, w, lax.rem(mine + d, groups))

    near_slot = fi * NEAR + other
    take(near_slot)
    for h in range(heads):
        absorb(h, near_slot)

    def from_far(i):
        for h in range(heads):
            absorb(h, far_peer(i + 1)[0] * NEAR + ni)
    each(far - 1, from_far)

    def across(i):
        s = far_peer(i + 1)[0] * NEAR + other
        take(s)
        for h in range(heads):
            absorb(h, s)
    each(far - 2, across)
    last = far_peer(far - 1)[0] * NEAR + other
    take(last)

    def out_to(h, d):
        g, peer = group_peer(d)
        return remote(ost.at[h, g], out_ref.at[mine, h], o_send.at[h, d], o_recv.at[h, mine], peer)

    partner = lax.rem(mi + 1, PAIR)

    def text_to(h):
        return remote(tst.at[h, partner], tout_ref.at[mi, h], t_sems.at[0, h], t_sems.at[1, h],
                      at(fi, partner, ni, hd))

    for h in range(heads):
        absorb(h, last)
        result = (acc[h] / total[h]).astype(jnp.bfloat16)
        ost[h] = result[:rows].reshape(groups, tokens, dim)
        tst[h] = result[rows:].reshape(tst.shape[1:])
        for d in range(1, groups):
            out_to(h, d).start()
        text_to(h).start()
        out_ref[mine, h] = ost[h, mine]
        tout_ref[mi, h] = tst[h, mi]

    for d in range(1, groups):
        kv_to_group(0, d).wait_send()
        kv_to_group(1, d).wait_send()
        q_to_group(d).wait_send()
    for w in range(2):
        for d in range(groups):
            g = lax.rem(mine + d, groups)
            each(far - 1, lambda i: kv_to_far(w, g, i + 1).wait_send())
            each(far, lambda i: kv_to_near(far_peer(i)[0] * NEAR + ni, w, g, 1).wait_send())
    for h in range(heads):
        for d in range(1, groups):
            g, peer = group_peer(d)
            out_to(h, d).wait_send()
            remote(ost.at[h, g], out_ref.at[g, h], o_send.at[h, d], o_recv.at[h, g], peer).wait_recv()
        text_to(h).wait_send()
        remote(tst.at[h, partner], tout_ref.at[partner, h], t_sems.at[0, h], t_sems.at[1, h],
               at(fi, partner, ni, hd)).wait_recv()


def local(ctxs, hds, video_q, video_k, video_v, positions, text_q, text_k, text_v, text_count):
    tokens, all_heads, dim = video_q.shape
    text = text_q.shape[0]
    groups = PAIR * hds
    heads = all_heads // groups
    far = ctxs // (PAIR * NEAR)
    share = text // ctxs
    rows = groups * tokens + PAIR * share
    axis, freq, swap = constants(dim)
    pos = positions.astype(jnp.float32)[:, :, None]
    lane_axis = axis[None, :]
    angle = jnp.where(lane_axis == 0, pos[0], jnp.where(lane_axis == 1, pos[1], pos[2])) * freq[None, :]
    cos, sin = jnp.cos(angle), jnp.sin(angle)

    def by_head(x):
        return jnp.swapaxes(x, 0, 1).reshape(groups, heads, tokens, dim)

    ctx = lax.axis_index("ctx")
    fi, mi, ni = ctx // (PAIR * NEAR), (ctx // NEAR) % PAIR, ctx % NEAR

    def text_heads(x):
        return jnp.swapaxes(lax.dynamic_slice_in_dim(x, mi * heads, heads, 1), 0, 1)

    tq = text_q.reshape(far, PAIR, NEAR, share, PAIR * heads, dim)
    tq = lax.dynamic_slice(tq, (fi, 0, ni, 0, mi * heads, 0), (1, PAIR, 1, share, heads, dim))
    tq = jnp.swapaxes(tq.reshape(PAIR * share, heads, dim), 0, 1)
    vmem = pl.BlockSpec(memory_space=pltpu.VMEM)
    dma = pltpu.SemaphoreType.DMA
    slots = far * NEAR
    out, tout = pl.pallas_call(
        functools.partial(kernel, far, hds),
        name="joint_attention",
        out_shape=(
            jax.ShapeDtypeStruct((groups, heads, tokens, dim), jnp.bfloat16),
            jax.ShapeDtypeStruct((PAIR, heads, share, dim), jnp.bfloat16),
        ),
        in_specs=[vmem] * 9 + [pl.BlockSpec(memory_space=pltpu.SMEM)],
        out_specs=(vmem, vmem),
        scratch_shapes=[
            pltpu.VMEM((groups, heads, tokens, dim), jnp.bfloat16),
            pltpu.VMEM((groups, heads, tokens, dim), jnp.bfloat16),
            pltpu.VMEM((groups, heads, tokens, dim), jnp.bfloat16),
            pltpu.VMEM((slots, 2, groups, heads, tokens, dim), jnp.bfloat16),
            pltpu.VMEM((heads, groups, tokens, dim), jnp.bfloat16),
            pltpu.VMEM((heads, PAIR, share, dim), jnp.bfloat16),
            pltpu.VMEM((heads, rows, dim), jnp.float32),
            pltpu.VMEM((heads, rows, 1), jnp.float32),
            pltpu.VMEM((heads, rows, 1), jnp.float32),
            dma((3, groups)),
            dma((groups,)),
            dma((slots, 2, groups)),
            dma((far, 2, groups)),
            dma((far, 2, groups)),
            dma((heads, groups)),
            dma((heads, groups)),
            dma((2, heads)),
        ],
        compiler_params=pltpu.CompilerParams(
            collective_id=0, has_side_effects=True, vmem_limit_bytes=60 * 1024 * 1024
        ),
    )(
        by_head(video_q), by_head(video_k), by_head(video_v), cos, sin, jnp.asarray(swap, jnp.bfloat16),
        tq, text_heads(text_k), text_heads(text_v), text_count,
    )
    video_out = jnp.swapaxes(out.reshape(all_heads, tokens, dim), 0, 1)
    text_out = jnp.swapaxes(tout.reshape(PAIR * heads, share, dim), 0, 1)
    return (video_out, text_out)


def solution(mesh):
    return jax.shard_map(
        functools.partial(local, mesh.shape["ctx"], mesh.shape["hd"]),
        mesh=mesh,
        in_specs=(
            P(("ctx", "hd"), "grp", None),
            P(("ctx", "hd"), "grp", None),
            P(("ctx", "hd"), "grp", None),
            P(None, ("ctx", "hd")),
            P(None, ("grp", "hd"), None),
            P(None, ("grp", "hd"), None),
            P(None, ("grp", "hd"), None),
            P(),
        ),
        out_specs=(P(("ctx", "hd"), "grp", None), P("ctx", ("grp", "hd"), None)),
        check_vma=False,
    )
```

```python
import functools
import math

import jax
import jax.numpy as jnp
import numpy as np
from jax import lax
from jax.experimental import pallas as pl
from jax.experimental.pallas import tpu as pltpu
from jax.sharding import PartitionSpec as P

THETA = 256.0
MESH = pl.DeviceIdType.MESH
PAIR = 2
NEAR = 2


def bands(dim):
    band_t = dim // 8
    band_h = (dim - band_t) // 2
    return (band_t, band_h, dim - band_t - band_h)


def constants(dim):
    freq = np.zeros((dim,), np.float32)
    swap = np.zeros((dim, dim), np.float32)
    start = 0
    for size in bands(dim):
        half = size // 2
        for i in range(half):
            low, high = start + i, start + half + i
            freq[low] = freq[high] = np.float32(THETA ** (-2.0 * i / size))
            swap[high, low] = -1.0
            swap[low, high] = 1.0
        start += size
    return freq, swap


def each(count, body):
    if count <= 4:
        for i in range(count):
            body(i)
    else:
        lax.fori_loop(0, count, lambda i, _: (body(i), 0)[1], 0)


def kernel(far, hds, q_ref, k_ref, v_ref, tq_ref, tk_ref, tv_ref, pos_ref, freq_ref, swap_ref, count_ref,
           out_ref, tout_ref, qin, kin, tqs, tks, tvs, qs, ks, qg, kv, ost, tst, acc, peak, total, probs,
           in_sems, a_send, q_recv, kv_recv, f_send, n_send, o_send, o_recv, t_sems):
    ctx = lax.axis_index("ctx")
    hd = lax.axis_index("hd")
    fi, mi, ni = ctx // (PAIR * NEAR), (ctx // NEAR) % PAIR, ctx % NEAR
    groups = PAIR * hds
    heads = v_ref.shape[1]
    tokens, dim = v_ref.shape[2], v_ref.shape[3]
    mine = hd * PAIR + mi
    slot = fi * NEAR + ni

    def at(f, m, n, h):
        return {"ctx": (f * PAIR + m) * NEAR + n, "hd": h}

    def group_peer(d):
        g = lax.rem(mine + d, groups)
        return g, at(fi, g % PAIR, ni, g // PAIR)

    def far_peer(d):
        f = lax.rem(fi + d, far)
        return f, at(f, mi, ni, hd)

    def near_peer(d):
        n = lax.rem(ni + d, NEAR)
        return n, at(fi, mi, n, hd)

    text_heads = pl.ds(mi * heads, heads)
    k_in = pltpu.make_async_copy(k_ref, kin, in_sems.at[0])
    q_in = pltpu.make_async_copy(q_ref, qin, in_sems.at[1])
    v_in = pltpu.make_async_copy(v_ref.at[mine], kv.at[slot, 1, mine], in_sems.at[2])
    text_in = (
        pltpu.make_async_copy(tq_ref.at[text_heads], tqs, in_sems.at[3]),
        pltpu.make_async_copy(tk_ref.at[text_heads], tks, in_sems.at[4]),
        pltpu.make_async_copy(tv_ref.at[text_heads], tvs, in_sems.at[5]),
    )
    for copy in (k_in, q_in, v_in) + text_in:
        copy.start()
    barrier = pltpu.get_barrier_semaphore()

    def greet(peer):
        pl.semaphore_signal(barrier, inc=1, device_id=peer, device_id_type=MESH)

    each(groups - 1, lambda i: greet(group_peer(i + 1)[1]))
    each(far - 1, lambda i: greet(far_peer(i + 1)[1]))
    each(NEAR - 1, lambda i: greet(near_peer(i + 1)[1]))

    swap = swap_ref[...]
    diagonal = (lax.broadcasted_iota(jnp.int32, (tokens, tokens), 0)
                == lax.broadcasted_iota(jnp.int32, (tokens, tokens), 1))
    lane = lax.broadcasted_iota(jnp.int32, (tokens, dim), 1)

    def column(axis):
        row = pos_ref[axis:axis + 1, :].astype(jnp.float32)
        return jnp.sum(jnp.where(diagonal, row, 0.0), axis=1, keepdims=True)

    band_t, band_h, _ = bands(dim)
    angle = jnp.where(lane < band_t, column(0), jnp.where(lane < band_t + band_h, column(1), column(2))) * freq_ref[...]
    cos, sin = jnp.cos(angle), jnp.sin(angle)

    def rotate(src, dst):
        for g in range(groups):
            for h in range(heads):
                x = src[g, h]
                turned = jnp.dot(x, swap, preferred_element_type=jnp.float32)
                dst[g, h] = (x.astype(jnp.float32) * cos + turned * sin).astype(jnp.bfloat16)

    k_in.wait()
    rotate(kin, ks)
    q_in.wait()
    rotate(qin, qs)
    kv[slot, 0, mine] = ks[mine]
    qg[mine] = qs[mine]
    v_in.wait()
    pl.semaphore_wait(barrier, (groups - 1) + (far - 1) + (NEAR - 1))

    def remote(src, dst, send, recv, peer):
        return pltpu.make_async_remote_copy(src_ref=src, dst_ref=dst, send_sem=send, recv_sem=recv,
                                            device_id=peer, device_id_type=MESH)

    def kv_to_group(w, d):
        g, peer = group_peer(d)
        src = ks if w == 0 else v_ref
        return remote(src.at[g], kv.at[slot, w, mine], a_send.at[w, d], kv_recv.at[slot, w, mine], peer)

    def q_to_group(d):
        g, peer = group_peer(d)
        return remote(qs.at[g], qg.at[mine], a_send.at[2, d], q_recv.at[mine], peer)

    def kv_to_far(w, g, d):
        f, peer = far_peer(d)
        piece = kv.at[slot, w, g]
        return remote(piece, piece, f_send.at[d, w, g], kv_recv.at[slot, w, g], peer)

    def kv_to_near(s, w, g, d):
        n, peer = near_peer(d)
        piece = kv.at[s, w, g]
        return remote(piece, piece, n_send.at[s // NEAR, w, g], kv_recv.at[s, w, g], peer)

    def arrived(s, w, g):
        piece = kv.at[s, w, g]
        remote(piece, piece, n_send.at[0, w, g], kv_recv.at[s, w, g], near_peer(1)[1]).wait_recv()

    def spread(w, g):
        each(far - 1, lambda i: kv_to_far(w, g, i + 1).start())
        kv_to_near(slot, w, g, 1).start()

    for w in range(2):
        for d in range(1, groups):
            kv_to_group(w, d).start()
        spread(w, mine)
    for d in range(1, groups):
        q_to_group(d).start()
    for w in range(2):
        for d in range(1, groups):
            g = lax.rem(mine + d, groups)
            arrived(slot, w, g)
            spread(w, g)

    scale = math.log2(math.e) / math.sqrt(dim)
    rows = groups * tokens

    def queries(h):
        own_text = [tqs[h, (fi * PAIR + m) * NEAR + ni] for m in range(PAIR)]
        return jnp.concatenate([qg[:, h].reshape(rows, dim)] + own_text, axis=0)

    def score(h, keys):
        return lax.dot_general(queries(h), keys, (((1,), (1,)), ((), ())), preferred_element_type=jnp.float32) * scale

    for d in range(1, groups):
        g = lax.rem(mine + d, groups)
        remote(qg.at[g], qg.at[g], a_send.at[2, d], q_recv.at[g], group_peer(d)[1]).wait_recv()
    for copy in text_in:
        copy.wait()

    def start_text():
        for h in range(heads):
            s = score(h, tks[h])
            live = lax.broadcasted_iota(jnp.int32, s.shape, 1) < count_ref[0]
            s = jnp.where(live, s, -jnp.inf)
            top = jnp.max(s, axis=1, keepdims=True)
            p = jnp.exp2(s - top)
            peak[h] = top
            total[h] = jnp.sum(p, axis=1, keepdims=True)
            acc[h] = jnp.dot(p.astype(jnp.bfloat16), tvs[h], preferred_element_type=jnp.float32)

    def keys_of(s, h):
        return kv[s, 0, :, h].reshape(rows, dim)

    def values_of(s, h):
        return kv[s, 1, :, h].reshape(rows, dim)

    def weigh(h, keys):
        sc = score(h, keys)
        old = peak[h]
        top = jnp.maximum(old, jnp.max(sc, axis=1, keepdims=True))
        p = jnp.exp2(sc - top)
        factor = jnp.exp2(old - top)
        peak[h] = top
        total[h] = total[h] * factor + jnp.sum(p, axis=1, keepdims=True)
        return p.astype(jnp.bfloat16), factor

    def absorb(s):
        for h in range(heads):
            p, factor = weigh(h, keys_of(s, h))
            acc[h] = acc[h] * factor + jnp.dot(p, values_of(s, h), preferred_element_type=jnp.float32)

    other = near_peer(1)[0]
    near_slot = fi * NEAR + other

    def from_far(i):
        f = far_peer(i + 1)[0]
        return f * NEAR + ni, f * NEAR + other

    def relay(i, w, d):
        s, g = from_far(i)[0], lax.rem(mine + d, groups)
        arrived(s, w, g)
        kv_to_near(s, w, g, 1).start()

    def take(s, w):
        for d in range(groups):
            arrived(s, w, lax.rem(mine + d, groups))

    def whole(i):
        for w in range(2):
            for d in range(groups):
                relay(i, w, d)
        straight, across = from_far(i)
        absorb(straight)
        take(across, 0)
        take(across, 1)
        absorb(across)

    start_text()
    each(far - 2, whole)
    last = far - 2
    straight, across = from_far(last)
    relay(last, 0, 0)
    relay(last, 1, 0)
    absorb(slot)
    for d in range(1, groups):
        relay(last, 0, d)
    take(near_slot, 0)
    take(near_slot, 1)
    absorb(near_slot)
    relay(last, 1, 1)
    take(across, 0)
    for h in range(heads):
        p, factor = weigh(h, jnp.concatenate([keys_of(straight, h), keys_of(across, h)], axis=0))
        probs[h] = p
        acc[h] = acc[h] * factor
    for d in range(2, groups):
        relay(last, 1, d)
    for h in range(heads):
        acc[h] += jnp.dot(probs[h, :, :rows], values_of(straight, h), preferred_element_type=jnp.float32)
    take(across, 1)

    def out_to(h, d):
        g, peer = group_peer(d)
        return remote(ost.at[h, g], out_ref.at[mine, h], o_send.at[h, d], o_recv.at[h, mine], peer)

    partner = lax.rem(mi + 1, PAIR)

    def text_to(h):
        return remote(tst.at[h, partner], tout_ref.at[mi, h], t_sems.at[0, h], t_sems.at[1, h],
                      at(fi, partner, ni, hd))

    for h in range(heads):
        mixed = acc[h] + jnp.dot(probs[h, :, rows:], values_of(across, h), preferred_element_type=jnp.float32)
        result = (mixed / total[h]).astype(jnp.bfloat16)
        ost[h] = result[:rows].reshape(groups, tokens, dim)
        tst[h] = result[rows:].reshape(tst.shape[1:])
        for d in range(1, groups):
            out_to(h, d).start()
        text_to(h).start()
        out_ref[mine, h] = ost[h, mine]
        tout_ref[mi, h] = tst[h, mi]

    for d in range(1, groups):
        kv_to_group(0, d).wait_send()
        kv_to_group(1, d).wait_send()
        q_to_group(d).wait_send()
    for w in range(2):
        for d in range(groups):
            g = lax.rem(mine + d, groups)
            each(far - 1, lambda i: kv_to_far(w, g, i + 1).wait_send())
            each(far, lambda i: kv_to_near(far_peer(i)[0] * NEAR + ni, w, g, 1).wait_send())
    for h in range(heads):
        for d in range(1, groups):
            g, peer = group_peer(d)
            out_to(h, d).wait_send()
            remote(ost.at[h, g], out_ref.at[g, h], o_send.at[h, d], o_recv.at[h, g], peer).wait_recv()
        text_to(h).wait_send()
        remote(tst.at[h, partner], tout_ref.at[partner, h], t_sems.at[0, h], t_sems.at[1, h],
               at(fi, partner, ni, hd)).wait_recv()


def local(ctxs, hds, video_q, video_k, video_v, positions, text_q, text_k, text_v, text_count):
    tokens, all_heads, dim = video_q.shape
    text = text_q.shape[0]
    groups = PAIR * hds
    heads = all_heads // groups
    far = ctxs // (PAIR * NEAR)
    share = text // ctxs
    rows = groups * tokens + PAIR * share
    freq, swap = constants(dim)

    def by_head(x):
        return jnp.swapaxes(x, 0, 1).reshape(groups, heads, tokens, dim)

    vmem = pl.BlockSpec(memory_space=pltpu.VMEM)
    dma = pltpu.SemaphoreType.DMA
    slots = far * NEAR
    out, tout = pl.pallas_call(
        functools.partial(kernel, far, hds),
        name="joint_attention",
        out_shape=(
            jax.ShapeDtypeStruct((groups, heads, tokens, dim), jnp.bfloat16),
            jax.ShapeDtypeStruct((PAIR, heads, share, dim), jnp.bfloat16),
        ),
        in_specs=[pl.BlockSpec(memory_space=pl.ANY)] * 6 + [vmem] * 3 + [pl.BlockSpec(memory_space=pltpu.SMEM)],
        out_specs=(vmem, vmem),
        scratch_shapes=[
            pltpu.VMEM((groups, heads, tokens, dim), jnp.bfloat16),
            pltpu.VMEM((groups, heads, tokens, dim), jnp.bfloat16),
            pltpu.VMEM((heads, ctxs, share, dim), jnp.bfloat16),
            pltpu.VMEM((heads, text, dim), jnp.bfloat16),
            pltpu.VMEM((heads, text, dim), jnp.bfloat16),
            pltpu.VMEM((groups, heads, tokens, dim), jnp.bfloat16),
            pltpu.VMEM((groups, heads, tokens, dim), jnp.bfloat16),
            pltpu.VMEM((groups, heads, tokens, dim), jnp.bfloat16),
            pltpu.VMEM((slots, 2, groups, heads, tokens, dim), jnp.bfloat16),
            pltpu.VMEM((heads, groups, tokens, dim), jnp.bfloat16),
            pltpu.VMEM((heads, PAIR, share, dim), jnp.bfloat16),
            pltpu.VMEM((heads, rows, dim), jnp.float32),
            pltpu.VMEM((heads, rows, 1), jnp.float32),
            pltpu.VMEM((heads, rows, 1), jnp.float32),
            pltpu.VMEM((heads, rows, 2 * groups * tokens), jnp.bfloat16),
            dma((6,)),
            dma((3, groups)),
            dma((groups,)),
            dma((slots, 2, groups)),
            dma((far, 2, groups)),
            dma((far, 2, groups)),
            dma((heads, groups)),
            dma((heads, groups)),
            dma((2, heads)),
        ],
        compiler_params=pltpu.CompilerParams(
            collective_id=0, has_side_effects=True, vmem_limit_bytes=60 * 1024 * 1024
        ),
    )(
        by_head(video_q), by_head(video_k), by_head(video_v),
        jnp.swapaxes(text_q, 0, 1).reshape(PAIR * heads, ctxs, share, dim), jnp.swapaxes(text_k, 0, 1), jnp.swapaxes(text_v, 0, 1),
        positions, jnp.asarray(freq[None, :]), jnp.asarray(swap, jnp.bfloat16), text_count,
    )
    video_out = jnp.swapaxes(out.reshape(all_heads, tokens, dim), 0, 1)
    text_out = jnp.swapaxes(tout.reshape(PAIR * heads, share, dim), 0, 1)
    return (video_out, text_out)


def solution(mesh):
    return jax.shard_map(
        functools.partial(local, mesh.shape["ctx"], mesh.shape["hd"]),
        mesh=mesh,
        in_specs=(
            P(("ctx", "hd"), "grp", None),
            P(("ctx", "hd"), "grp", None),
            P(("ctx", "hd"), "grp", None),
            P(None, ("ctx", "hd")),
            P(None, ("grp", "hd"), None),
            P(None, ("grp", "hd"), None),
            P(None, ("grp", "hd"), None),
            P(),
        ),
        out_specs=(P(("ctx", "hd"), "grp", None), P("ctx", ("grp", "hd"), None)),
        check_vma=False,
    )
```

```python
import functools
import math

import jax
import jax.numpy as jnp
import numpy as np
from jax import lax
from jax.experimental import pallas as pl
from jax.experimental.pallas import tpu as pltpu
from jax.sharding import PartitionSpec as P

THETA = 256.0
MESH = pl.DeviceIdType.MESH
PAIR = 2
NEAR = 2


def bands(dim):
    band_t = dim // 8
    band_h = (dim - band_t) // 2
    return (band_t, band_h, dim - band_t - band_h)


def constants(dim):
    freq = np.zeros((dim,), np.float32)
    swap = np.zeros((dim, dim), np.float32)
    start = 0
    for size in bands(dim):
        half = size // 2
        for i in range(half):
            low, high = start + i, start + half + i
            freq[low] = freq[high] = np.float32(THETA ** (-2.0 * i / size))
            swap[high, low] = -1.0
            swap[low, high] = 1.0
        start += size
    return freq, swap


def each(count, body):
    if count <= 4:
        for i in range(count):
            body(i)
    else:
        lax.fori_loop(0, count, lambda i, _: (body(i), 0)[1], 0)


def kernel(far, hds, q_ref, k_ref, v_ref, tq_ref, tk_ref, tv_ref, pos_ref, freq_ref, swap_ref, count_ref,
           out_ref, tout_ref, qin, kin, tqs, tks, tvs, qs, ks, qg, kv, ost, tst, acc, peak, total, probs,
           in_sems, a_send, q_recv, kv_recv, f_send, n_send, o_send, o_recv, t_sems):
    ctx = lax.axis_index("ctx")
    hd = lax.axis_index("hd")
    fi, mi, ni = ctx // (PAIR * NEAR), (ctx // NEAR) % PAIR, ctx % NEAR
    groups = PAIR * hds
    heads = v_ref.shape[1]
    tokens, dim = v_ref.shape[2], v_ref.shape[3]
    mine = hd * PAIR + mi
    slot = fi * NEAR + ni

    def at(f, m, n, h):
        return {"ctx": (f * PAIR + m) * NEAR + n, "hd": h}

    def group_peer(d):
        g = lax.rem(mine + d, groups)
        return g, at(fi, g % PAIR, ni, g // PAIR)

    def far_peer(d):
        f = lax.rem(fi + d, far)
        return f, at(f, mi, ni, hd)

    def near_peer(d):
        n = lax.rem(ni + d, NEAR)
        return n, at(fi, mi, n, hd)

    text_heads = pl.ds(mi * heads, heads)
    k_in = pltpu.make_async_copy(k_ref, kin, in_sems.at[0])
    q_in = pltpu.make_async_copy(q_ref, qin, in_sems.at[1])
    v_in = pltpu.make_async_copy(v_ref.at[mine], kv.at[slot, 1, mine], in_sems.at[2])
    text_in = (
        pltpu.make_async_copy(tq_ref.at[text_heads], tqs, in_sems.at[3]),
        pltpu.make_async_copy(tk_ref.at[text_heads], tks, in_sems.at[4]),
        pltpu.make_async_copy(tv_ref.at[text_heads], tvs, in_sems.at[5]),
    )
    for copy in (k_in, q_in, v_in) + text_in:
        copy.start()
    barrier = pltpu.get_barrier_semaphore()

    def greet(peer):
        pl.semaphore_signal(barrier, inc=1, device_id=peer, device_id_type=MESH)

    each(groups - 1, lambda i: greet(group_peer(i + 1)[1]))
    each(far - 1, lambda i: greet(far_peer(i + 1)[1]))
    each(NEAR - 1, lambda i: greet(near_peer(i + 1)[1]))

    swap = swap_ref[...]
    diagonal = (lax.broadcasted_iota(jnp.int32, (tokens, tokens), 0)
                == lax.broadcasted_iota(jnp.int32, (tokens, tokens), 1))
    lane = lax.broadcasted_iota(jnp.int32, (tokens, dim), 1)

    def column(axis):
        row = pos_ref[axis:axis + 1, :].astype(jnp.float32)
        return jnp.sum(jnp.where(diagonal, row, 0.0), axis=1, keepdims=True)

    band_t, band_h, _ = bands(dim)
    angle = jnp.where(lane < band_t, column(0), jnp.where(lane < band_t + band_h, column(1), column(2))) * freq_ref[...]
    cos, sin = jnp.cos(angle), jnp.sin(angle)

    def rotate(src, dst):
        for g in range(groups):
            for h in range(heads):
                x = src[g, h]
                turned = jnp.dot(x, swap, preferred_element_type=jnp.float32)
                dst[g, h] = (x.astype(jnp.float32) * cos + turned * sin).astype(jnp.bfloat16)

    k_in.wait()
    rotate(kin, ks)
    q_in.wait()
    rotate(qin, qs)
    kv[slot, 0, mine] = ks[mine]
    qg[mine] = qs[mine]
    v_in.wait()
    pl.semaphore_wait(barrier, (groups - 1) + (far - 1) + (NEAR - 1))

    def remote(src, dst, send, recv, peer):
        return pltpu.make_async_remote_copy(src_ref=src, dst_ref=dst, send_sem=send, recv_sem=recv,
                                            device_id=peer, device_id_type=MESH)

    def kv_to_group(w, d):
        g, peer = group_peer(d)
        src = ks if w == 0 else v_ref
        return remote(src.at[g], kv.at[slot, w, mine], a_send.at[w, d], kv_recv.at[slot, w, mine], peer)

    def q_to_group(d):
        g, peer = group_peer(d)
        return remote(qs.at[g], qg.at[mine], a_send.at[2, d], q_recv.at[mine], peer)

    def kv_to_far(w, g, d):
        f, peer = far_peer(d)
        piece = kv.at[slot, w, g]
        return remote(piece, piece, f_send.at[d, w, g], kv_recv.at[slot, w, g], peer)

    def kv_to_near(s, w, g, d):
        n, peer = near_peer(d)
        piece = kv.at[s, w, g]
        return remote(piece, piece, n_send.at[s // NEAR, w, g], kv_recv.at[s, w, g], peer)

    def arrived(s, w, g):
        piece = kv.at[s, w, g]
        remote(piece, piece, n_send.at[0, w, g], kv_recv.at[s, w, g], near_peer(1)[1]).wait_recv()

    def spread(w, g):
        each(far - 1, lambda i: kv_to_far(w, g, i + 1).start())
        kv_to_near(slot, w, g, 1).start()

    for w in range(2):
        for d in range(1, groups):
            kv_to_group(w, d).start()
    for d in range(1, groups):
        q_to_group(d).start()
    for w in range(2):
        spread(w, mine)
    for w in range(2):
        for d in range(1, groups):
            g = lax.rem(mine + d, groups)
            arrived(slot, w, g)
            spread(w, g)

    scale = math.log2(math.e) / math.sqrt(dim)
    rows = groups * tokens

    def queries(h):
        own_text = [tqs[h, (fi * PAIR + m) * NEAR + ni] for m in range(PAIR)]
        return jnp.concatenate([qg[:, h].reshape(rows, dim)] + own_text, axis=0)

    def score(h, keys):
        return lax.dot_general(queries(h), keys, (((1,), (1,)), ((), ())), preferred_element_type=jnp.float32) * scale

    for d in range(1, groups):
        g = lax.rem(mine + d, groups)
        remote(qg.at[g], qg.at[g], a_send.at[2, d], q_recv.at[g], group_peer(d)[1]).wait_recv()
    for copy in text_in:
        copy.wait()

    def start_text():
        for h in range(heads):
            s = score(h, tks[h])
            live = lax.broadcasted_iota(jnp.int32, s.shape, 1) < count_ref[0]
            s = jnp.where(live, s, -jnp.inf)
            top = jnp.max(s, axis=1, keepdims=True)
            p = jnp.exp2(s - top)
            peak[h] = top
            total[h] = jnp.sum(p, axis=1, keepdims=True)
            acc[h] = jnp.dot(p.astype(jnp.bfloat16), tvs[h], preferred_element_type=jnp.float32)

    def keys_of(s, h):
        return kv[s, 0, :, h].reshape(rows, dim)

    def values_of(s, h):
        return kv[s, 1, :, h].reshape(rows, dim)

    def weigh(h, keys):
        sc = score(h, keys)
        old = peak[h]
        top = jnp.maximum(old, jnp.max(sc, axis=1, keepdims=True))
        p = jnp.exp2(sc - top)
        factor = jnp.exp2(old - top)
        peak[h] = top
        total[h] = total[h] * factor + jnp.sum(p, axis=1, keepdims=True)
        return p.astype(jnp.bfloat16), factor

    def absorb(s):
        for h in range(heads):
            p, factor = weigh(h, keys_of(s, h))
            acc[h] = acc[h] * factor + jnp.dot(p, values_of(s, h), preferred_element_type=jnp.float32)

    other = near_peer(1)[0]
    near_slot = fi * NEAR + other

    def from_far(i):
        f = far_peer(i + 1)[0]
        return f * NEAR + ni, f * NEAR + other

    def relay(i, w, d):
        s, g = from_far(i)[0], lax.rem(mine + d, groups)
        arrived(s, w, g)
        kv_to_near(s, w, g, 1).start()

    def take(s, w):
        for d in range(groups):
            arrived(s, w, lax.rem(mine + d, groups))

    def whole(i):
        for w in range(2):
            for d in range(groups):
                relay(i, w, d)
        straight, across = from_far(i)
        absorb(straight)
        take(across, 0)
        take(across, 1)
        absorb(across)

    start_text()
    each(far - 2, whole)
    last = far - 2
    straight, across = from_far(last)
    relay(last, 0, 0)
    relay(last, 1, 0)
    absorb(slot)
    for d in range(1, groups):
        relay(last, 0, d)
    take(near_slot, 0)
    take(near_slot, 1)
    absorb(near_slot)
    relay(last, 1, 1)
    take(across, 0)
    for h in range(heads):
        p, factor = weigh(h, jnp.concatenate([keys_of(straight, h), keys_of(across, h)], axis=0))
        probs[h] = p
        acc[h] = acc[h] * factor
    for d in range(2, groups):
        relay(last, 1, d)
    for h in range(heads):
        acc[h] += jnp.dot(probs[h, :, :rows], values_of(straight, h), preferred_element_type=jnp.float32)
    take(across, 1)

    def out_to(h, d):
        g, peer = group_peer(d)
        return remote(ost.at[h, g], out_ref.at[mine, h], o_send.at[h, d], o_recv.at[h, mine], peer)

    partner = lax.rem(mi + 1, PAIR)

    def text_to(h):
        return remote(tst.at[h, partner], tout_ref.at[mi, h], t_sems.at[0, h], t_sems.at[1, h],
                      at(fi, partner, ni, hd))

    for h in range(heads):
        mixed = acc[h] + jnp.dot(probs[h, :, rows:], values_of(across, h), preferred_element_type=jnp.float32)
        result = (mixed / total[h]).astype(jnp.bfloat16)
        ost[h] = result[:rows].reshape(groups, tokens, dim)
        tst[h] = result[rows:].reshape(tst.shape[1:])
        for d in range(1, groups):
            out_to(h, d).start()
        text_to(h).start()
        out_ref[mine, h] = ost[h, mine]
        tout_ref[mi, h] = tst[h, mi]

    for d in range(1, groups):
        kv_to_group(0, d).wait_send()
        kv_to_group(1, d).wait_send()
        q_to_group(d).wait_send()
    for w in range(2):
        for d in range(groups):
            g = lax.rem(mine + d, groups)
            each(far - 1, lambda i: kv_to_far(w, g, i + 1).wait_send())
            each(far, lambda i: kv_to_near(far_peer(i)[0] * NEAR + ni, w, g, 1).wait_send())
    for h in range(heads):
        for d in range(1, groups):
            g, peer = group_peer(d)
            out_to(h, d).wait_send()
            remote(ost.at[h, g], out_ref.at[g, h], o_send.at[h, d], o_recv.at[h, g], peer).wait_recv()
        text_to(h).wait_send()
        remote(tst.at[h, partner], tout_ref.at[partner, h], t_sems.at[0, h], t_sems.at[1, h],
               at(fi, partner, ni, hd)).wait_recv()


def settle(out_ref, tout_ref, video_ref, text_ref):
    video_ref[...] = out_ref[...]
    text_ref[...] = tout_ref[...]


def local(ctxs, hds, video_q, video_k, video_v, positions, text_q, text_k, text_v, text_count):
    tokens, all_heads, dim = video_q.shape
    text = text_q.shape[0]
    groups = PAIR * hds
    heads = all_heads // groups
    far = ctxs // (PAIR * NEAR)
    share = text // ctxs
    rows = groups * tokens + PAIR * share
    freq, swap = constants(dim)

    def by_head(x):
        return jnp.swapaxes(x, 0, 1).reshape(groups, heads, tokens, dim)

    vmem = pl.BlockSpec(memory_space=pltpu.VMEM)
    dma = pltpu.SemaphoreType.DMA
    slots = far * NEAR
    out, tout = pl.pallas_call(
        functools.partial(kernel, far, hds),
        name="joint_attention",
        out_shape=(
            jax.ShapeDtypeStruct((groups, heads, tokens, dim), jnp.bfloat16),
            jax.ShapeDtypeStruct((PAIR, heads, share, dim), jnp.bfloat16),
        ),
        in_specs=[pl.BlockSpec(memory_space=pl.ANY)] * 6 + [vmem] * 3 + [pl.BlockSpec(memory_space=pltpu.SMEM)],
        out_specs=(vmem, vmem),
        scratch_shapes=[
            pltpu.VMEM((groups, heads, tokens, dim), jnp.bfloat16),
            pltpu.VMEM((groups, heads, tokens, dim), jnp.bfloat16),
            pltpu.VMEM((heads, ctxs, share, dim), jnp.bfloat16),
            pltpu.VMEM((heads, text, dim), jnp.bfloat16),
            pltpu.VMEM((heads, text, dim), jnp.bfloat16),
            pltpu.VMEM((groups, heads, tokens, dim), jnp.bfloat16),
            pltpu.VMEM((groups, heads, tokens, dim), jnp.bfloat16),
            pltpu.VMEM((groups, heads, tokens, dim), jnp.bfloat16),
            pltpu.VMEM((slots, 2, groups, heads, tokens, dim), jnp.bfloat16),
            pltpu.VMEM((heads, groups, tokens, dim), jnp.bfloat16),
            pltpu.VMEM((heads, PAIR, share, dim), jnp.bfloat16),
            pltpu.VMEM((heads, rows, dim), jnp.float32),
            pltpu.VMEM((heads, rows, 1), jnp.float32),
            pltpu.VMEM((heads, rows, 1), jnp.float32),
            pltpu.VMEM((heads, rows, 2 * groups * tokens), jnp.bfloat16),
            dma((6,)),
            dma((3, groups)),
            dma((groups,)),
            dma((slots, 2, groups)),
            dma((far, 2, groups)),
            dma((far, 2, groups)),
            dma((heads, groups)),
            dma((heads, groups)),
            dma((2, heads)),
        ],
        compiler_params=pltpu.CompilerParams(
            collective_id=0, has_side_effects=True, vmem_limit_bytes=60 * 1024 * 1024
        ),
    )(
        by_head(video_q), by_head(video_k), by_head(video_v),
        jnp.swapaxes(text_q, 0, 1).reshape(PAIR * heads, ctxs, share, dim), jnp.swapaxes(text_k, 0, 1), jnp.swapaxes(text_v, 0, 1),
        positions, jnp.asarray(freq[None, :]), jnp.asarray(swap, jnp.bfloat16), text_count,
    )
    out, tout = pl.pallas_call(
        settle,
        name="settle",
        out_shape=(jax.ShapeDtypeStruct(out.shape, out.dtype), jax.ShapeDtypeStruct(tout.shape, tout.dtype)),
        in_specs=[vmem] * 2,
        out_specs=(vmem, vmem),
    )(out, tout)
    video_out = jnp.swapaxes(out.reshape(all_heads, tokens, dim), 0, 1)
    text_out = jnp.swapaxes(tout.reshape(PAIR * heads, share, dim), 0, 1)
    return (video_out, text_out)


def solution(mesh):
    return jax.shard_map(
        functools.partial(local, mesh.shape["ctx"], mesh.shape["hd"]),
        mesh=mesh,
        in_specs=(
            P(("ctx", "hd"), "grp", None),
            P(("ctx", "hd"), "grp", None),
            P(("ctx", "hd"), "grp", None),
            P(None, ("ctx", "hd")),
            P(None, ("grp", "hd"), None),
            P(None, ("grp", "hd"), None),
            P(None, ("grp", "hd"), None),
            P(),
        ),
        out_specs=(P(("ctx", "hd"), "grp", None), P("ctx", ("grp", "hd"), None)),
        check_vma=False,
    )
```

```python
import functools
import math

import jax
import jax.numpy as jnp
import numpy as np
from jax import lax
from jax.experimental import pallas as pl
from jax.experimental.pallas import tpu as pltpu
from jax.sharding import PartitionSpec as P

THETA = 256.0
MESH = pl.DeviceIdType.MESH
PAIR = 2
NEAR = 2


def bands(dim):
    band_t = dim // 8
    band_h = (dim - band_t) // 2
    return (band_t, band_h, dim - band_t - band_h)


def constants(dim):
    freq = np.zeros((dim,), np.float32)
    swap = np.zeros((dim, dim), np.float32)
    start = 0
    for size in bands(dim):
        half = size // 2
        for i in range(half):
            low, high = start + i, start + half + i
            freq[low] = freq[high] = np.float32(THETA ** (-2.0 * i / size))
            swap[high, low] = -1.0
            swap[low, high] = 1.0
        start += size
    return freq, swap


def each(count, body):
    if count <= 4:
        for i in range(count):
            body(i)
    else:
        lax.fori_loop(0, count, lambda i, _: (body(i), 0)[1], 0)


def kernel(far, hds, q_ref, k_ref, v_ref, tq_ref, tk_ref, tv_ref, pos_in, freq_in, swap_in, count_ref,
           out_ref, tout_ref, pos_ref, freq_ref, swap_ref, qin, kin, tqs, tks, tvs, qs, ks, qg, kv, ost, tst, acc, peak, total, probs,
           in_sems, a_send, q_recv, kv_recv, f_send, n_send, o_send, o_recv, t_sems):
    ctx = lax.axis_index("ctx")
    hd = lax.axis_index("hd")
    fi, mi, ni = ctx // (PAIR * NEAR), (ctx // NEAR) % PAIR, ctx % NEAR
    groups = PAIR * hds
    heads = v_ref.shape[1]
    tokens, dim = v_ref.shape[2], v_ref.shape[3]
    mine = hd * PAIR + mi
    slot = fi * NEAR + ni

    def at(f, m, n, h):
        return {"ctx": (f * PAIR + m) * NEAR + n, "hd": h}

    def group_of(d):
        return lax.rem(hd + d // PAIR, hds) * PAIR + lax.rem(mi + d % PAIR, PAIR)

    def group_peer(d):
        g = group_of(d)
        return g, at(fi, g % PAIR, ni, g // PAIR)

    straight_first = [d for d in range(PAIR, groups, PAIR)]
    rest = [d for d in range(1, groups) if d % PAIR]
    early = [(0, 0), (1, 0)] + [(w, d) for d in straight_first for w in range(2)] + [(0, d) for d in rest]
    late = [(1, d) for d in rest]

    def far_peer(d):
        f = lax.rem(fi + d, far)
        return f, at(f, mi, ni, hd)

    def near_peer(d):
        n = lax.rem(ni + d, NEAR)
        return n, at(fi, mi, n, hd)

    text_heads = pl.ds(mi * heads, heads)
    k_in = pltpu.make_async_copy(k_ref, kin, in_sems.at[0])
    q_in = pltpu.make_async_copy(q_ref, qin, in_sems.at[1])
    v_in = pltpu.make_async_copy(v_ref.at[mine], kv.at[slot, 1, mine], in_sems.at[2])
    text_in = (
        pltpu.make_async_copy(tq_ref.at[text_heads], tqs, in_sems.at[3]),
        pltpu.make_async_copy(tk_ref.at[text_heads], tks, in_sems.at[4]),
        pltpu.make_async_copy(tv_ref.at[text_heads], tvs, in_sems.at[5]),
    )
    table_in = (
        pltpu.make_async_copy(pos_in, pos_ref, in_sems.at[6]),
        pltpu.make_async_copy(freq_in, freq_ref, in_sems.at[7]),
        pltpu.make_async_copy(swap_in, swap_ref, in_sems.at[8]),
    )
    barrier = pltpu.get_barrier_semaphore()

    def greet(peer):
        pl.semaphore_signal(barrier, inc=1, device_id=peer, device_id_type=MESH)

    each(groups - 1, lambda i: greet(group_peer(i + 1)[1]))
    each(far - 1, lambda i: greet(far_peer(i + 1)[1]))
    each(NEAR - 1, lambda i: greet(near_peer(i + 1)[1]))

    for copy in table_in + (k_in, q_in, v_in) + text_in:
        copy.start()
    for copy in table_in:
        copy.wait()
    swap = swap_ref[...]
    diagonal = (lax.broadcasted_iota(jnp.int32, (tokens, tokens), 0)
                == lax.broadcasted_iota(jnp.int32, (tokens, tokens), 1))
    lane = lax.broadcasted_iota(jnp.int32, (tokens, dim), 1)

    def column(axis):
        row = pos_ref[axis:axis + 1, :].astype(jnp.float32)
        return jnp.sum(jnp.where(diagonal, row, 0.0), axis=1, keepdims=True)

    band_t, band_h, _ = bands(dim)
    angle = jnp.where(lane < band_t, column(0), jnp.where(lane < band_t + band_h, column(1), column(2))) * freq_ref[...]
    cos, sin = jnp.cos(angle), jnp.sin(angle)

    def rotate(src, dst):
        for g in range(groups):
            for h in range(heads):
                x = src[g, h]
                turned = jnp.dot(x, swap, preferred_element_type=jnp.float32)
                dst[g, h] = (x.astype(jnp.float32) * cos + turned * sin).astype(jnp.bfloat16)

    k_in.wait()
    rotate(kin, ks)
    q_in.wait()
    rotate(qin, qs)
    kv[slot, 0, mine] = ks[mine]
    qg[mine] = qs[mine]
    v_in.wait()
    pl.semaphore_wait(barrier, (groups - 1) + (far - 1) + (NEAR - 1))

    def remote(src, dst, send, recv, peer):
        return pltpu.make_async_remote_copy(src_ref=src, dst_ref=dst, send_sem=send, recv_sem=recv,
                                            device_id=peer, device_id_type=MESH)

    def kv_to_group(w, d):
        g, peer = group_peer(d)
        src = ks if w == 0 else v_ref
        return remote(src.at[g], kv.at[slot, w, mine], a_send.at[w, d], kv_recv.at[slot, w, mine], peer)

    def q_to_group(d):
        g, peer = group_peer(d)
        return remote(qs.at[g], qg.at[mine], a_send.at[2, d], q_recv.at[mine], peer)

    def kv_to_far(w, g, d):
        f, peer = far_peer(d)
        piece = kv.at[slot, w, g]
        return remote(piece, piece, f_send.at[d, w, g], kv_recv.at[slot, w, g], peer)

    def kv_to_near(s, w, g, d):
        n, peer = near_peer(d)
        piece = kv.at[s, w, g]
        return remote(piece, piece, n_send.at[s // NEAR, w, g], kv_recv.at[s, w, g], peer)

    def arrived(s, w, g):
        piece = kv.at[s, w, g]
        remote(piece, piece, n_send.at[0, w, g], kv_recv.at[s, w, g], near_peer(1)[1]).wait_recv()

    def spread(w, g):
        each(far - 1, lambda i: kv_to_far(w, g, i + 1).start())
        kv_to_near(slot, w, g, 1).start()

    for w, d in (early + late)[2:]:
        kv_to_group(w, d).start()
    for d in straight_first + rest:
        q_to_group(d).start()
    for w in range(2):
        spread(w, mine)
    for w, d in (early + late)[2:]:
        g = group_of(d)
        arrived(slot, w, g)
        spread(w, g)

    scale = math.log2(math.e) / math.sqrt(dim)
    rows = groups * tokens

    def queries(h):
        own_text = [tqs[h, (fi * PAIR + m) * NEAR + ni] for m in range(PAIR)]
        return jnp.concatenate([qg[:, h].reshape(rows, dim)] + own_text, axis=0)

    def score(h, keys):
        return lax.dot_general(queries(h), keys, (((1,), (1,)), ((), ())), preferred_element_type=jnp.float32) * scale

    for d in range(1, groups):
        g = group_of(d)
        remote(qg.at[g], qg.at[g], a_send.at[2, d], q_recv.at[g], group_peer(d)[1]).wait_recv()
    for copy in text_in:
        copy.wait()

    def start_text():
        for h in range(heads):
            s = score(h, tks[h])
            live = lax.broadcasted_iota(jnp.int32, s.shape, 1) < count_ref[0]
            s = jnp.where(live, s, -jnp.inf)
            top = jnp.max(s, axis=1, keepdims=True)
            p = jnp.exp2(s - top)
            peak[h] = top
            total[h] = jnp.sum(p, axis=1, keepdims=True)
            acc[h] = jnp.dot(p.astype(jnp.bfloat16), tvs[h], preferred_element_type=jnp.float32)

    def keys_of(s, h):
        return kv[s, 0, :, h].reshape(rows, dim)

    def values_of(s, h):
        return kv[s, 1, :, h].reshape(rows, dim)

    def weigh(h, keys):
        sc = score(h, keys)
        old = peak[h]
        top = jnp.maximum(old, jnp.max(sc, axis=1, keepdims=True))
        p = jnp.exp2(sc - top)
        factor = jnp.exp2(old - top)
        peak[h] = top
        total[h] = total[h] * factor + jnp.sum(p, axis=1, keepdims=True)
        return p.astype(jnp.bfloat16), factor

    def absorb(s):
        for h in range(heads):
            p, factor = weigh(h, keys_of(s, h))
            acc[h] = acc[h] * factor + jnp.dot(p, values_of(s, h), preferred_element_type=jnp.float32)

    other = near_peer(1)[0]
    near_slot = fi * NEAR + other

    def from_far(i):
        f = far_peer(i + 1)[0]
        return f * NEAR + ni, f * NEAR + other

    def relay(i, w, d):
        s, g = from_far(i)[0], group_of(d)
        arrived(s, w, g)
        kv_to_near(s, w, g, 1).start()

    def take(s, w):
        for d in range(groups):
            arrived(s, w, group_of(d))

    def whole(i):
        for w, d in early + late:
            relay(i, w, d)
        straight, across = from_far(i)
        absorb(straight)
        take(across, 0)
        take(across, 1)
        absorb(across)

    start_text()
    each(far - 2, whole)
    last = far - 2
    straight, across = from_far(last)
    relay(last, 0, 0)
    relay(last, 1, 0)
    absorb(slot)
    for w, d in early[2:]:
        relay(last, w, d)
    take(near_slot, 0)
    take(near_slot, 1)
    absorb(near_slot)
    take(across, 0)
    for h in range(heads):
        p, factor = weigh(h, jnp.concatenate([keys_of(straight, h), keys_of(across, h)], axis=0))
        probs[h] = p
        acc[h] = acc[h] * factor
    for w, d in late:
        relay(last, w, d)
    for h in range(heads):
        acc[h] += jnp.dot(probs[h, :, :rows], values_of(straight, h), preferred_element_type=jnp.float32)
    take(across, 1)

    def out_to(h, d):
        g, peer = group_peer(d)
        return remote(ost.at[h, g], out_ref.at[mine, h], o_send.at[h, d], o_recv.at[h, mine], peer)

    partner = lax.rem(mi + 1, PAIR)

    def text_to(h):
        return remote(tst.at[h, partner], tout_ref.at[mi, h], t_sems.at[0, h], t_sems.at[1, h],
                      at(fi, partner, ni, hd))

    for h in range(heads):
        mixed = acc[h] + jnp.dot(probs[h, :, rows:], values_of(across, h), preferred_element_type=jnp.float32)
        result = (mixed / total[h]).astype(jnp.bfloat16)
        ost[h] = result[:rows].reshape(groups, tokens, dim)
        tst[h] = result[rows:].reshape(tst.shape[1:])
        for d in range(1, groups):
            out_to(h, d).start()
        text_to(h).start()
        out_ref[mine, h] = ost[h, mine]
        tout_ref[mi, h] = tst[h, mi]

    for d in range(1, groups):
        kv_to_group(0, d).wait_send()
        kv_to_group(1, d).wait_send()
        q_to_group(d).wait_send()
    for w in range(2):
        for d in range(groups):
            g = group_of(d)
            each(far - 1, lambda i: kv_to_far(w, g, i + 1).wait_send())
            each(far, lambda i: kv_to_near(far_peer(i)[0] * NEAR + ni, w, g, 1).wait_send())
    for h in range(heads):
        for d in range(1, groups):
            g, peer = group_peer(d)
            out_to(h, d).wait_send()
            remote(ost.at[h, g], out_ref.at[g, h], o_send.at[h, d], o_recv.at[h, g], peer).wait_recv()
        text_to(h).wait_send()
        remote(tst.at[h, partner], tout_ref.at[partner, h], t_sems.at[0, h], t_sems.at[1, h],
               at(fi, partner, ni, hd)).wait_recv()


def settle(out_ref, tout_ref, video_ref, text_ref):
    video_ref[...] = out_ref[...]
    text_ref[...] = tout_ref[...]


def local(ctxs, hds, video_q, video_k, video_v, positions, text_q, text_k, text_v, text_count):
    tokens, all_heads, dim = video_q.shape
    text = text_q.shape[0]
    groups = PAIR * hds
    heads = all_heads // groups
    far = ctxs // (PAIR * NEAR)
    share = text // ctxs
    rows = groups * tokens + PAIR * share
    freq, swap = constants(dim)

    def by_head(x):
        return jnp.swapaxes(x, 0, 1).reshape(groups, heads, tokens, dim)

    vmem = pl.BlockSpec(memory_space=pltpu.VMEM)
    dma = pltpu.SemaphoreType.DMA
    slots = far * NEAR
    room = 12 * 2**20 + slots * 2 * all_heads * tokens * dim * 3
    out, tout = pl.pallas_call(
        functools.partial(kernel, far, hds),
        name="joint_attention",
        out_shape=(
            jax.ShapeDtypeStruct((groups, heads, tokens, dim), jnp.bfloat16),
            jax.ShapeDtypeStruct((PAIR, heads, share, dim), jnp.bfloat16),
        ),
        in_specs=[pl.BlockSpec(memory_space=pltpu.HBM)] * 9 + [pl.BlockSpec(memory_space=pltpu.SMEM)],
        out_specs=(vmem, vmem),
        scratch_shapes=[
            pltpu.VMEM(positions.shape, jnp.int32),
            pltpu.VMEM((1, dim), jnp.float32),
            pltpu.VMEM((dim, dim), jnp.bfloat16),
            pltpu.VMEM((groups, heads, tokens, dim), jnp.bfloat16),
            pltpu.VMEM((groups, heads, tokens, dim), jnp.bfloat16),
            pltpu.VMEM((heads, ctxs, share, dim), jnp.bfloat16),
            pltpu.VMEM((heads, text, dim), jnp.bfloat16),
            pltpu.VMEM((heads, text, dim), jnp.bfloat16),
            pltpu.VMEM((groups, heads, tokens, dim), jnp.bfloat16),
            pltpu.VMEM((groups, heads, tokens, dim), jnp.bfloat16),
            pltpu.VMEM((groups, heads, tokens, dim), jnp.bfloat16),
            pltpu.VMEM((slots, 2, groups, heads, tokens, dim), jnp.bfloat16),
            pltpu.VMEM((heads, groups, tokens, dim), jnp.bfloat16),
            pltpu.VMEM((heads, PAIR, share, dim), jnp.bfloat16),
            pltpu.VMEM((heads, rows, dim), jnp.float32),
            pltpu.VMEM((heads, rows, 1), jnp.float32),
            pltpu.VMEM((heads, rows, 1), jnp.float32),
            pltpu.VMEM((heads, rows, 2 * groups * tokens), jnp.bfloat16),
            dma((9,)),
            dma((3, groups)),
            dma((groups,)),
            dma((slots, 2, groups)),
            dma((far, 2, groups)),
            dma((far, 2, groups)),
            dma((heads, groups)),
            dma((heads, groups)),
            dma((2, heads)),
        ],
        compiler_params=pltpu.CompilerParams(
            collective_id=0, has_side_effects=True, vmem_limit_bytes=room
        ),
    )(
        by_head(video_q), by_head(video_k), by_head(video_v),
        jnp.swapaxes(text_q, 0, 1).reshape(PAIR * heads, ctxs, share, dim), jnp.swapaxes(text_k, 0, 1), jnp.swapaxes(text_v, 0, 1),
        positions, jnp.asarray(freq[None, :]), jnp.asarray(swap, jnp.bfloat16), text_count,
    )
    out, tout = pl.pallas_call(
        settle,
        name="settle",
        out_shape=(jax.ShapeDtypeStruct(out.shape, out.dtype), jax.ShapeDtypeStruct(tout.shape, tout.dtype)),
        in_specs=[vmem] * 2,
        out_specs=(vmem, vmem),
        compiler_params=pltpu.CompilerParams(vmem_limit_bytes=4 * 2**20),
    )(out, tout)
    video_out = jnp.swapaxes(out.reshape(all_heads, tokens, dim), 0, 1)
    text_out = jnp.swapaxes(tout.reshape(PAIR * heads, share, dim), 0, 1)
    return (video_out, text_out)


def solution(mesh):
    return jax.shard_map(
        functools.partial(local, mesh.shape["ctx"], mesh.shape["hd"]),
        mesh=mesh,
        in_specs=(
            P(("ctx", "hd"), "grp", None),
            P(("ctx", "hd"), "grp", None),
            P(("ctx", "hd"), "grp", None),
            P(None, ("ctx", "hd")),
            P(None, ("grp", "hd"), None),
            P(None, ("grp", "hd"), None),
            P(None, ("grp", "hd"), None),
            P(),
        ),
        out_specs=(P(("ctx", "hd"), "grp", None), P("ctx", ("grp", "hd"), None)),
        check_vma=False,
    )
```

```python
import functools
import math

import jax
import jax.numpy as jnp
import numpy as np
from jax import lax
from jax.experimental import pallas as pl
from jax.experimental.pallas import tpu as pltpu
from jax.sharding import PartitionSpec as P

THETA = 256.0
MESH = pl.DeviceIdType.MESH
PAIR = 2
NEAR = 2


def bands(dim):
    band_t = dim // 8
    band_h = (dim - band_t) // 2
    return (band_t, band_h, dim - band_t - band_h)


def constants(dim):
    freq = np.zeros((dim,), np.float32)
    swap = np.zeros((dim, dim), np.float32)
    start = 0
    for size in bands(dim):
        half = size // 2
        for i in range(half):
            low, high = start + i, start + half + i
            freq[low] = freq[high] = np.float32(THETA ** (-2.0 * i / size))
            swap[high, low] = -1.0
            swap[low, high] = 1.0
        start += size
    return freq, swap


def each(count, body):
    if count <= 4:
        for i in range(count):
            body(i)
    else:
        lax.fori_loop(0, count, lambda i, _: (body(i), 0)[1], 0)


def kernel(far, hds, q_ref, k_ref, v_ref, tq_ref, tk_ref, tv_ref, pos_in, freq_in, swap_in, count_ref,
           out_ref, tout_ref, pos_ref, freq_ref, swap_ref, qin, kin, tqs, tks, tvs, qs, ks, qg, kv, ost, tst, acc, peak, total, probs,
           in_sems, a_send, q_recv, kv_recv, f_send, n_send, o_send, o_recv, t_sems):
    ctx = lax.axis_index("ctx")
    hd = lax.axis_index("hd")
    fi, mi, ni = ctx // (PAIR * NEAR), (ctx // NEAR) % PAIR, ctx % NEAR
    groups = PAIR * hds
    heads = v_ref.shape[1]
    tokens, dim = v_ref.shape[2], v_ref.shape[3]
    mine = hd * PAIR + mi
    slot = fi * NEAR + ni

    def at(f, m, n, h):
        return {"ctx": (f * PAIR + m) * NEAR + n, "hd": h}

    def group_of(d):
        return lax.rem(hd + d // PAIR, hds) * PAIR + lax.rem(mi + d % PAIR, PAIR)

    def group_peer(d):
        g = group_of(d)
        return g, at(fi, g % PAIR, ni, g // PAIR)

    straight_first = [d for d in range(PAIR, groups, PAIR)]
    rest = [d for d in range(1, groups) if d % PAIR]
    early = [(0, 0), (1, 0)] + [(w, d) for d in straight_first for w in range(2)] + [(0, d) for d in rest]
    late = [(1, d) for d in rest]

    def far_peer(d):
        f = lax.rem(fi + d, far)
        return f, at(f, mi, ni, hd)

    def near_peer(d):
        n = lax.rem(ni + d, NEAR)
        return n, at(fi, mi, n, hd)

    text_heads = pl.ds(mi * heads, heads)
    k_in = pltpu.make_async_copy(k_ref, kin, in_sems.at[0])
    q_in = pltpu.make_async_copy(q_ref, qin, in_sems.at[1])
    v_in = pltpu.make_async_copy(v_ref.at[mine], kv.at[slot, 1, mine], in_sems.at[2])
    text_in = (
        pltpu.make_async_copy(tq_ref.at[text_heads], tqs, in_sems.at[3]),
        pltpu.make_async_copy(tk_ref.at[text_heads], tks, in_sems.at[4]),
        pltpu.make_async_copy(tv_ref.at[text_heads], tvs, in_sems.at[5]),
    )
    table_in = (
        pltpu.make_async_copy(pos_in, pos_ref, in_sems.at[6]),
        pltpu.make_async_copy(freq_in, freq_ref, in_sems.at[7]),
        pltpu.make_async_copy(swap_in, swap_ref, in_sems.at[8]),
    )
    barrier = pltpu.get_barrier_semaphore()

    def greet(peer):
        pl.semaphore_signal(barrier, inc=1, device_id=peer, device_id_type=MESH)

    each(groups - 1, lambda i: greet(group_peer(i + 1)[1]))
    each(far - 1, lambda i: greet(far_peer(i + 1)[1]))
    each(NEAR - 1, lambda i: greet(near_peer(i + 1)[1]))

    for copy in table_in + (k_in, q_in, v_in) + text_in:
        copy.start()
    for copy in table_in:
        copy.wait()
    swap = swap_ref[...]
    diagonal = (lax.broadcasted_iota(jnp.int32, (tokens, tokens), 0)
                == lax.broadcasted_iota(jnp.int32, (tokens, tokens), 1))
    lane = lax.broadcasted_iota(jnp.int32, (tokens, dim), 1)

    def column(axis):
        row = pos_ref[axis:axis + 1, :].astype(jnp.float32)
        return jnp.sum(jnp.where(diagonal, row, 0.0), axis=1, keepdims=True)

    band_t, band_h, _ = bands(dim)
    angle = jnp.where(lane < band_t, column(0), jnp.where(lane < band_t + band_h, column(1), column(2))) * freq_ref[...]
    cos, sin = jnp.cos(angle), jnp.sin(angle)

    def rotate(src, dst):
        for g in range(groups):
            for h in range(heads):
                x = src[g, h]
                turned = jnp.dot(x, swap, preferred_element_type=jnp.float32)
                dst[g, h] = (x.astype(jnp.float32) * cos + turned * sin).astype(jnp.bfloat16)

    k_in.wait()
    rotate(kin, ks)
    q_in.wait()
    rotate(qin, qs)
    kv[slot, 0, mine] = ks[mine]
    qg[mine] = qs[mine]
    v_in.wait()
    pl.semaphore_wait(barrier, (groups - 1) + (far - 1) + (NEAR - 1))

    def remote(src, dst, send, recv, peer):
        return pltpu.make_async_remote_copy(src_ref=src, dst_ref=dst, send_sem=send, recv_sem=recv,
                                            device_id=peer, device_id_type=MESH)

    def kv_to_group(w, d):
        g, peer = group_peer(d)
        src = ks if w == 0 else v_ref
        return remote(src.at[g], kv.at[slot, w, mine], a_send.at[w, d], kv_recv.at[slot, w, mine], peer)

    def q_to_group(d):
        g, peer = group_peer(d)
        return remote(qs.at[g], qg.at[mine], a_send.at[2, d], q_recv.at[mine], peer)

    def kv_to_far(w, g, d):
        f, peer = far_peer(d)
        piece = kv.at[slot, w, g]
        return remote(piece, piece, f_send.at[d, w, g], kv_recv.at[slot, w, g], peer)

    def kv_to_near(s, w, g, d):
        n, peer = near_peer(d)
        piece = kv.at[s, w, g]
        return remote(piece, piece, n_send.at[s // NEAR, w, g], kv_recv.at[s, w, g], peer)

    def arrived(s, w, g):
        piece = kv.at[s, w, g]
        remote(piece, piece, n_send.at[0, w, g], kv_recv.at[s, w, g], near_peer(1)[1]).wait_recv()

    def spread(w, g):
        each(far - 1, lambda i: kv_to_far(w, g, i + 1).start())
        kv_to_near(slot, w, g, 1).start()

    for w, d in (early + late)[2:]:
        kv_to_group(w, d).start()
    for w in range(2):
        spread(w, mine)
    for d in straight_first + rest:
        q_to_group(d).start()
    for w, d in (early + late)[2:]:
        g = group_of(d)
        arrived(slot, w, g)
        spread(w, g)

    scale = math.log2(math.e) / math.sqrt(dim)
    rows = groups * tokens

    def queries(h):
        own_text = [tqs[h, (fi * PAIR + m) * NEAR + ni] for m in range(PAIR)]
        return jnp.concatenate([qg[:, h].reshape(rows, dim)] + own_text, axis=0)

    def score(h, keys):
        return lax.dot_general(queries(h), keys, (((1,), (1,)), ((), ())), preferred_element_type=jnp.float32) * scale

    for d in range(1, groups):
        g = group_of(d)
        remote(qg.at[g], qg.at[g], a_send.at[2, d], q_recv.at[g], group_peer(d)[1]).wait_recv()
    for copy in text_in:
        copy.wait()

    def start_text():
        for h in range(heads):
            s = score(h, tks[h])
            live = lax.broadcasted_iota(jnp.int32, s.shape, 1) < count_ref[0]
            s = jnp.where(live, s, -jnp.inf)
            top = jnp.max(s, axis=1, keepdims=True)
            p = jnp.exp2(s - top)
            peak[h] = top
            total[h] = jnp.sum(p, axis=1, keepdims=True)
            acc[h] = jnp.dot(p.astype(jnp.bfloat16), tvs[h], preferred_element_type=jnp.float32)

    def keys_of(s, h):
        return kv[s, 0, :, h].reshape(rows, dim)

    def values_of(s, h):
        return kv[s, 1, :, h].reshape(rows, dim)

    def weigh(h, keys):
        sc = score(h, keys)
        old = peak[h]
        top = jnp.maximum(old, jnp.max(sc, axis=1, keepdims=True))
        p = jnp.exp2(sc - top)
        factor = jnp.exp2(old - top)
        peak[h] = top
        total[h] = total[h] * factor + jnp.sum(p, axis=1, keepdims=True)
        return p.astype(jnp.bfloat16), factor

    def absorb(s):
        for h in range(heads):
            p, factor = weigh(h, keys_of(s, h))
            acc[h] = acc[h] * factor + jnp.dot(p, values_of(s, h), preferred_element_type=jnp.float32)

    other = near_peer(1)[0]
    near_slot = fi * NEAR + other

    def from_far(i):
        f = far_peer(i + 1)[0]
        return f * NEAR + ni, f * NEAR + other

    def relay(i, w, d):
        s, g = from_far(i)[0], group_of(d)
        arrived(s, w, g)
        kv_to_near(s, w, g, 1).start()

    def take(s, w):
        for d in range(groups):
            arrived(s, w, group_of(d))

    def whole(i):
        for w, d in early + late:
            relay(i, w, d)
        straight, across = from_far(i)
        absorb(straight)
        take(across, 0)
        take(across, 1)
        absorb(across)

    start_text()
    each(far - 2, whole)
    last = far - 2
    straight, across = from_far(last)
    relay(last, 0, 0)
    relay(last, 1, 0)
    absorb(slot)
    for w, d in early[2:]:
        relay(last, w, d)
    take(near_slot, 0)
    take(near_slot, 1)
    absorb(near_slot)
    take(across, 0)
    for h in range(heads):
        p, factor = weigh(h, jnp.concatenate([keys_of(straight, h), keys_of(across, h)], axis=0))
        probs[h] = p
        acc[h] = acc[h] * factor
    for w, d in late:
        relay(last, w, d)
    for h in range(heads):
        acc[h] += jnp.dot(probs[h, :, :rows], values_of(straight, h), preferred_element_type=jnp.float32)
    take(across, 1)

    def out_to(h, d):
        g, peer = group_peer(d)
        return remote(ost.at[h, g], out_ref.at[mine, h], o_send.at[h, d], o_recv.at[h, mine], peer)

    partner = lax.rem(mi + 1, PAIR)

    def text_to(h):
        return remote(tst.at[h, partner], tout_ref.at[mi, h], t_sems.at[0, h], t_sems.at[1, h],
                      at(fi, partner, ni, hd))

    for h in range(heads):
        mixed = acc[h] + jnp.dot(probs[h, :, rows:], values_of(across, h), preferred_element_type=jnp.float32)
        result = (mixed / total[h]).astype(jnp.bfloat16)
        ost[h] = result[:rows].reshape(groups, tokens, dim)
        tst[h] = result[rows:].reshape(tst.shape[1:])
        for d in range(1, groups):
            out_to(h, d).start()
        text_to(h).start()
        out_ref[mine, h] = ost[h, mine]
        tout_ref[mi, h] = tst[h, mi]

    for d in range(1, groups):
        kv_to_group(0, d).wait_send()
        kv_to_group(1, d).wait_send()
        q_to_group(d).wait_send()
    for w in range(2):
        for d in range(groups):
            g = group_of(d)
            each(far - 1, lambda i: kv_to_far(w, g, i + 1).wait_send())
            each(far, lambda i: kv_to_near(far_peer(i)[0] * NEAR + ni, w, g, 1).wait_send())
    for h in range(heads):
        for d in range(1, groups):
            g, peer = group_peer(d)
            out_to(h, d).wait_send()
            remote(ost.at[h, g], out_ref.at[g, h], o_send.at[h, d], o_recv.at[h, g], peer).wait_recv()
        text_to(h).wait_send()
        remote(tst.at[h, partner], tout_ref.at[partner, h], t_sems.at[0, h], t_sems.at[1, h],
               at(fi, partner, ni, hd)).wait_recv()


def settle(out_ref, tout_ref, video_ref, text_ref):
    video_ref[...] = out_ref[...]
    text_ref[...] = tout_ref[...]


def local(ctxs, hds, video_q, video_k, video_v, positions, text_q, text_k, text_v, text_count):
    tokens, all_heads, dim = video_q.shape
    text = text_q.shape[0]
    groups = PAIR * hds
    heads = all_heads // groups
    far = ctxs // (PAIR * NEAR)
    share = text // ctxs
    rows = groups * tokens + PAIR * share
    freq, swap = constants(dim)

    def by_head(x):
        return jnp.swapaxes(x, 0, 1).reshape(groups, heads, tokens, dim)

    vmem = pl.BlockSpec(memory_space=pltpu.VMEM)
    dma = pltpu.SemaphoreType.DMA
    slots = far * NEAR
    out, tout = pl.pallas_call(
        functools.partial(kernel, far, hds),
        name="joint_attention",
        out_shape=(
            jax.ShapeDtypeStruct((groups, heads, tokens, dim), jnp.bfloat16),
            jax.ShapeDtypeStruct((PAIR, heads, share, dim), jnp.bfloat16),
        ),
        in_specs=[pl.BlockSpec(memory_space=pl.ANY)] * 9 + [pl.BlockSpec(memory_space=pltpu.SMEM)],
        out_specs=(vmem, vmem),
        scratch_shapes=[
            pltpu.VMEM(positions.shape, jnp.int32),
            pltpu.VMEM((1, dim), jnp.float32),
            pltpu.VMEM((dim, dim), jnp.bfloat16),
            pltpu.VMEM((groups, heads, tokens, dim), jnp.bfloat16),
            pltpu.VMEM((groups, heads, tokens, dim), jnp.bfloat16),
            pltpu.VMEM((heads, ctxs, share, dim), jnp.bfloat16),
            pltpu.VMEM((heads, text, dim), jnp.bfloat16),
            pltpu.VMEM((heads, text, dim), jnp.bfloat16),
            pltpu.VMEM((groups, heads, tokens, dim), jnp.bfloat16),
            pltpu.VMEM((groups, heads, tokens, dim), jnp.bfloat16),
            pltpu.VMEM((groups, heads, tokens, dim), jnp.bfloat16),
            pltpu.VMEM((slots, 2, groups, heads, tokens, dim), jnp.bfloat16),
            pltpu.VMEM((heads, groups, tokens, dim), jnp.bfloat16),
            pltpu.VMEM((heads, PAIR, share, dim), jnp.bfloat16),
            pltpu.VMEM((heads, rows, dim), jnp.float32),
            pltpu.VMEM((heads, rows, 1), jnp.float32),
            pltpu.VMEM((heads, rows, 1), jnp.float32),
            pltpu.VMEM((heads, rows, 2 * groups * tokens), jnp.bfloat16),
            dma((9,)),
            dma((3, groups)),
            dma((groups,)),
            dma((slots, 2, groups)),
            dma((far, 2, groups)),
            dma((far, 2, groups)),
            dma((heads, groups)),
            dma((heads, groups)),
            dma((2, heads)),
        ],
        compiler_params=pltpu.CompilerParams(
            collective_id=0, has_side_effects=True, vmem_limit_bytes=60 * 1024 * 1024
        ),
    )(
        by_head(video_q), by_head(video_k), by_head(video_v),
        jnp.swapaxes(text_q, 0, 1).reshape(PAIR * heads, ctxs, share, dim), jnp.swapaxes(text_k, 0, 1), jnp.swapaxes(text_v, 0, 1),
        positions, jnp.asarray(freq[None, :]), jnp.asarray(swap, jnp.bfloat16), text_count,
    )
    out, tout = pl.pallas_call(
        settle,
        name="settle",
        out_shape=(jax.ShapeDtypeStruct(out.shape, out.dtype), jax.ShapeDtypeStruct(tout.shape, tout.dtype)),
        in_specs=[vmem] * 2,
        out_specs=(vmem, vmem),
        compiler_params=pltpu.CompilerParams(vmem_limit_bytes=4 * 2**20),
    )(out, tout)
    video_out = jnp.swapaxes(out.reshape(all_heads, tokens, dim), 0, 1)
    text_out = jnp.swapaxes(tout.reshape(PAIR * heads, share, dim), 0, 1)
    return (video_out, text_out)


def solution(mesh):
    return jax.shard_map(
        functools.partial(local, mesh.shape["ctx"], mesh.shape["hd"]),
        mesh=mesh,
        in_specs=(
            P(("ctx", "hd"), "grp", None),
            P(("ctx", "hd"), "grp", None),
            P(("ctx", "hd"), "grp", None),
            P(None, ("ctx", "hd")),
            P(None, ("grp", "hd"), None),
            P(None, ("grp", "hd"), None),
            P(None, ("grp", "hd"), None),
            P(),
        ),
        out_specs=(P(("ctx", "hd"), "grp", None), P("ctx", ("grp", "hd"), None)),
        check_vma=False,
    )
```

```python
import functools
import math

import jax
import jax.numpy as jnp
import numpy as np
from jax import lax
from jax.experimental import pallas as pl
from jax.experimental.pallas import tpu as pltpu
from jax.sharding import PartitionSpec as P

THETA = 256.0
MESH = pl.DeviceIdType.MESH
PAIR = 2
NEAR = 2


def bands(dim):
    band_t = dim // 8
    band_h = (dim - band_t) // 2
    return (band_t, band_h, dim - band_t - band_h)


def constants(dim):
    freq = np.zeros((dim,), np.float32)
    swap = np.zeros((dim, dim), np.float32)
    start = 0
    for size in bands(dim):
        half = size // 2
        for i in range(half):
            low, high = start + i, start + half + i
            freq[low] = freq[high] = np.float32(THETA ** (-2.0 * i / size))
            swap[high, low] = -1.0
            swap[low, high] = 1.0
        start += size
    return freq, swap


def each(count, body):
    if count <= 4:
        for i in range(count):
            body(i)
    else:
        lax.fori_loop(0, count, lambda i, _: (body(i), 0)[1], 0)


def kernel(far, hds, q_ref, k_ref, v_ref, tq_ref, tk_ref, tv_ref, pos_in, freq_in, swap_in, count_ref,
           out_ref, tout_ref, pos_ref, freq_ref, swap_ref, qin, kin, tqs, tks, tvs, qs, ks, qg, kv, ost, tst, acc, peak, total, probs,
           in_sems, a_send, q_recv, kv_recv, f_send, n_send, o_send, o_recv, t_sems):
    ctx = lax.axis_index("ctx")
    hd = lax.axis_index("hd")
    fi, mi, ni = ctx // (PAIR * NEAR), (ctx // NEAR) % PAIR, ctx % NEAR
    groups = PAIR * hds
    heads = v_ref.shape[1]
    tokens, dim = v_ref.shape[2], v_ref.shape[3]
    mine = hd * PAIR + mi
    slot = fi * NEAR + ni

    def at(f, m, n, h):
        return {"ctx": (f * PAIR + m) * NEAR + n, "hd": h}

    def group_of(d):
        return lax.rem(hd + d // PAIR, hds) * PAIR + lax.rem(mi + d % PAIR, PAIR)

    def group_peer(d):
        g = group_of(d)
        return g, at(fi, g % PAIR, ni, g // PAIR)

    straight_first = [d for d in range(PAIR, groups, PAIR)]
    rest = [d for d in range(1, groups) if d % PAIR]
    early = [(0, 0), (1, 0)] + [(w, d) for d in straight_first for w in range(2)] + [(0, d) for d in rest]
    late = [(1, d) for d in rest]

    def far_peer(d):
        f = lax.rem(fi + d, far)
        return f, at(f, mi, ni, hd)

    def near_peer(d):
        n = lax.rem(ni + d, NEAR)
        return n, at(fi, mi, n, hd)

    text_heads = pl.ds(mi * heads, heads)
    k_in = pltpu.make_async_copy(k_ref, kin, in_sems.at[0])
    q_in = pltpu.make_async_copy(q_ref, qin, in_sems.at[1])
    v_in = pltpu.make_async_copy(v_ref.at[mine], kv.at[slot, 1, mine], in_sems.at[2])
    text_in = (
        pltpu.make_async_copy(tq_ref.at[text_heads], tqs, in_sems.at[3]),
        pltpu.make_async_copy(tk_ref.at[text_heads], tks, in_sems.at[4]),
        pltpu.make_async_copy(tv_ref.at[text_heads], tvs, in_sems.at[5]),
    )
    table_in = (
        pltpu.make_async_copy(pos_in, pos_ref, in_sems.at[6]),
        pltpu.make_async_copy(freq_in, freq_ref, in_sems.at[7]),
        pltpu.make_async_copy(swap_in, swap_ref, in_sems.at[8]),
    )
    barrier = pltpu.get_barrier_semaphore()

    def greet(peer):
        pl.semaphore_signal(barrier, inc=1, device_id=peer, device_id_type=MESH)

    each(groups - 1, lambda i: greet(group_peer(i + 1)[1]))
    each(far - 1, lambda i: greet(far_peer(i + 1)[1]))
    each(NEAR - 1, lambda i: greet(near_peer(i + 1)[1]))

    for copy in table_in + (k_in, q_in, v_in) + text_in:
        copy.start()
    for copy in table_in:
        copy.wait()
    swap = swap_ref[...]
    diagonal = (lax.broadcasted_iota(jnp.int32, (tokens, tokens), 0)
                == lax.broadcasted_iota(jnp.int32, (tokens, tokens), 1))
    lane = lax.broadcasted_iota(jnp.int32, (tokens, dim), 1)

    def column(axis):
        row = pos_ref[axis:axis + 1, :].astype(jnp.float32)
        return jnp.sum(jnp.where(diagonal, row, 0.0), axis=1, keepdims=True)

    band_t, band_h, _ = bands(dim)
    angle = jnp.where(lane < band_t, column(0), jnp.where(lane < band_t + band_h, column(1), column(2))) * freq_ref[...]
    cos, sin = jnp.cos(angle), jnp.sin(angle)

    def rotate(src, dst):
        for g in range(groups):
            for h in range(heads):
                x = src[g, h]
                turned = jnp.dot(x, swap, preferred_element_type=jnp.float32)
                dst[g, h] = (x.astype(jnp.float32) * cos + turned * sin).astype(jnp.bfloat16)

    k_in.wait()
    rotate(kin, ks)
    q_in.wait()
    rotate(qin, qs)
    kv[slot, 0, mine] = ks[mine]
    qg[mine] = qs[mine]
    v_in.wait()
    pl.semaphore_wait(barrier, (groups - 1) + (far - 1) + (NEAR - 1))

    def remote(src, dst, send, recv, peer):
        return pltpu.make_async_remote_copy(src_ref=src, dst_ref=dst, send_sem=send, recv_sem=recv,
                                            device_id=peer, device_id_type=MESH)

    def kv_to_group(w, d):
        g, peer = group_peer(d)
        src = ks if w == 0 else v_ref
        return remote(src.at[g], kv.at[slot, w, mine], a_send.at[w, d], kv_recv.at[slot, w, mine], peer)

    def q_to_group(d):
        g, peer = group_peer(d)
        return remote(qs.at[g], qg.at[mine], a_send.at[2, d], q_recv.at[mine], peer)

    def kv_to_far(w, g, d):
        f, peer = far_peer(d)
        piece = kv.at[slot, w, g]
        return remote(piece, piece, f_send.at[d, w, g], kv_recv.at[slot, w, g], peer)

    def kv_to_near(s, w, g, d):
        n, peer = near_peer(d)
        piece = kv.at[s, w, g]
        return remote(piece, piece, n_send.at[s // NEAR, w, g], kv_recv.at[s, w, g], peer)

    def arrived(s, w, g):
        piece = kv.at[s, w, g]
        remote(piece, piece, n_send.at[0, w, g], kv_recv.at[s, w, g], near_peer(1)[1]).wait_recv()

    def spread(w, g):
        each(far - 1, lambda i: kv_to_far(w, g, i + 1).start())
        kv_to_near(slot, w, g, 1).start()

    for w, d in (early + late)[2:]:
        kv_to_group(w, d).start()
    for d in straight_first + rest:
        q_to_group(d).start()
    for w in range(2):
        spread(w, mine)
    for w, d in (early + late)[2:]:
        g = group_of(d)
        arrived(slot, w, g)
        spread(w, g)

    scale = math.log2(math.e) / math.sqrt(dim)
    rows = groups * tokens

    def queries(h):
        own_text = [tqs[h, (fi * PAIR + m) * NEAR + ni] for m in range(PAIR)]
        return jnp.concatenate([qg[:, h].reshape(rows, dim)] + own_text, axis=0)

    def score(h, keys):
        return lax.dot_general(queries(h), keys, (((1,), (1,)), ((), ())), preferred_element_type=jnp.float32) * scale

    for d in range(1, groups):
        g = group_of(d)
        remote(qg.at[g], qg.at[g], a_send.at[2, d], q_recv.at[g], group_peer(d)[1]).wait_recv()
    for copy in text_in:
        copy.wait()

    def start_text():
        for h in range(heads):
            s = score(h, tks[h])
            live = lax.broadcasted_iota(jnp.int32, s.shape, 1) < count_ref[0]
            s = jnp.where(live, s, -jnp.inf)
            top = jnp.max(s, axis=1, keepdims=True)
            p = jnp.exp2(s - top)
            peak[h] = top
            total[h] = jnp.sum(p, axis=1, keepdims=True)
            acc[h] = jnp.dot(p.astype(jnp.bfloat16), tvs[h], preferred_element_type=jnp.float32)

    def keys_of(s, h):
        return kv[s, 0, :, h].reshape(rows, dim)

    def values_of(s, h):
        return kv[s, 1, :, h].reshape(rows, dim)

    def weigh(h, keys):
        sc = score(h, keys)
        old = peak[h]
        top = jnp.maximum(old, jnp.max(sc, axis=1, keepdims=True))
        p = jnp.exp2(sc - top)
        factor = jnp.exp2(old - top)
        peak[h] = top
        total[h] = total[h] * factor + jnp.sum(p, axis=1, keepdims=True)
        return p.astype(jnp.bfloat16), factor

    def absorb(s):
        for h in range(heads):
            p, factor = weigh(h, keys_of(s, h))
            acc[h] = acc[h] * factor + jnp.dot(p, values_of(s, h), preferred_element_type=jnp.float32)

    other = near_peer(1)[0]
    near_slot = fi * NEAR + other

    def from_far(i):
        f = far_peer(i + 1)[0]
        return f * NEAR + ni, f * NEAR + other

    def relay(i, w, d):
        s, g = from_far(i)[0], group_of(d)
        arrived(s, w, g)
        kv_to_near(s, w, g, 1).start()

    def take(s, w):
        for d in range(groups):
            arrived(s, w, group_of(d))

    def whole(i):
        for w, d in early + late:
            relay(i, w, d)
        straight, across = from_far(i)
        absorb(straight)
        take(across, 0)
        take(across, 1)
        absorb(across)

    start_text()
    each(far - 2, whole)
    last = far - 2
    straight, across = from_far(last)
    relay(last, 0, 0)
    relay(last, 1, 0)
    absorb(slot)
    for w, d in early[2:]:
        relay(last, w, d)
    take(near_slot, 0)
    take(near_slot, 1)
    absorb(near_slot)
    for w, d in late:
        relay(last, w, d)
    take(across, 0)
    for h in range(heads):
        p, factor = weigh(h, jnp.concatenate([keys_of(straight, h), keys_of(across, h)], axis=0))
        probs[h] = p
        acc[h] = acc[h] * factor
    for h in range(heads):
        acc[h] += jnp.dot(probs[h, :, :rows], values_of(straight, h), preferred_element_type=jnp.float32)
    take(across, 1)

    def out_to(h, d):
        g, peer = group_peer(d)
        return remote(ost.at[h, g], out_ref.at[mine, h], o_send.at[h, d], o_recv.at[h, mine], peer)

    partner = lax.rem(mi + 1, PAIR)

    def text_to(h):
        return remote(tst.at[h, partner], tout_ref.at[mi, h], t_sems.at[0, h], t_sems.at[1, h],
                      at(fi, partner, ni, hd))

    for h in range(heads):
        mixed = acc[h] + jnp.dot(probs[h, :, rows:], values_of(across, h), preferred_element_type=jnp.float32)
        result = (mixed / total[h]).astype(jnp.bfloat16)
        ost[h] = result[:rows].reshape(groups, tokens, dim)
        tst[h] = result[rows:].reshape(tst.shape[1:])
        for d in range(1, groups):
            out_to(h, d).start()
        text_to(h).start()
        out_ref[mine, h] = ost[h, mine]
        tout_ref[mi, h] = tst[h, mi]

    for d in range(1, groups):
        kv_to_group(0, d).wait_send()
        kv_to_group(1, d).wait_send()
        q_to_group(d).wait_send()
    for w in range(2):
        for d in range(groups):
            g = group_of(d)
            each(far - 1, lambda i: kv_to_far(w, g, i + 1).wait_send())
            each(far, lambda i: kv_to_near(far_peer(i)[0] * NEAR + ni, w, g, 1).wait_send())
    for h in range(heads):
        for d in range(1, groups):
            g, peer = group_peer(d)
            out_to(h, d).wait_send()
            remote(ost.at[h, g], out_ref.at[g, h], o_send.at[h, d], o_recv.at[h, g], peer).wait_recv()
        text_to(h).wait_send()
        remote(tst.at[h, partner], tout_ref.at[partner, h], t_sems.at[0, h], t_sems.at[1, h],
               at(fi, partner, ni, hd)).wait_recv()


def settle(out_ref, tout_ref, video_ref, text_ref):
    video_ref[...] = out_ref[...]
    text_ref[...] = tout_ref[...]


def local(ctxs, hds, video_q, video_k, video_v, positions, text_q, text_k, text_v, text_count):
    tokens, all_heads, dim = video_q.shape
    text = text_q.shape[0]
    groups = PAIR * hds
    heads = all_heads // groups
    far = ctxs // (PAIR * NEAR)
    share = text // ctxs
    rows = groups * tokens + PAIR * share
    freq, swap = constants(dim)

    def by_head(x):
        return jnp.swapaxes(x, 0, 1).reshape(groups, heads, tokens, dim)

    vmem = pl.BlockSpec(memory_space=pltpu.VMEM)
    dma = pltpu.SemaphoreType.DMA
    slots = far * NEAR
    out, tout = pl.pallas_call(
        functools.partial(kernel, far, hds),
        name="joint_attention",
        out_shape=(
            jax.ShapeDtypeStruct((groups, heads, tokens, dim), jnp.bfloat16),
            jax.ShapeDtypeStruct((PAIR, heads, share, dim), jnp.bfloat16),
        ),
        in_specs=[pl.BlockSpec(memory_space=pl.ANY)] * 9 + [pl.BlockSpec(memory_space=pltpu.SMEM)],
        out_specs=(vmem, vmem),
        scratch_shapes=[
            pltpu.VMEM(positions.shape, jnp.int32),
            pltpu.VMEM((1, dim), jnp.float32),
            pltpu.VMEM((dim, dim), jnp.bfloat16),
            pltpu.VMEM((groups, heads, tokens, dim), jnp.bfloat16),
            pltpu.VMEM((groups, heads, tokens, dim), jnp.bfloat16),
            pltpu.VMEM((heads, ctxs, share, dim), jnp.bfloat16),
            pltpu.VMEM((heads, text, dim), jnp.bfloat16),
            pltpu.VMEM((heads, text, dim), jnp.bfloat16),
            pltpu.VMEM((groups, heads, tokens, dim), jnp.bfloat16),
            pltpu.VMEM((groups, heads, tokens, dim), jnp.bfloat16),
            pltpu.VMEM((groups, heads, tokens, dim), jnp.bfloat16),
            pltpu.VMEM((slots, 2, groups, heads, tokens, dim), jnp.bfloat16),
            pltpu.VMEM((heads, groups, tokens, dim), jnp.bfloat16),
            pltpu.VMEM((heads, PAIR, share, dim), jnp.bfloat16),
            pltpu.VMEM((heads, rows, dim), jnp.float32),
            pltpu.VMEM((heads, rows, 1), jnp.float32),
            pltpu.VMEM((heads, rows, 1), jnp.float32),
            pltpu.VMEM((heads, rows, 2 * groups * tokens), jnp.bfloat16),
            dma((9,)),
            dma((3, groups)),
            dma((groups,)),
            dma((slots, 2, groups)),
            dma((far, 2, groups)),
            dma((far, 2, groups)),
            dma((heads, groups)),
            dma((heads, groups)),
            dma((2, heads)),
        ],
        compiler_params=pltpu.CompilerParams(
            collective_id=0, has_side_effects=True, vmem_limit_bytes=60 * 1024 * 1024
        ),
    )(
        by_head(video_q), by_head(video_k), by_head(video_v),
        jnp.swapaxes(text_q, 0, 1).reshape(PAIR * heads, ctxs, share, dim), jnp.swapaxes(text_k, 0, 1), jnp.swapaxes(text_v, 0, 1),
        positions, jnp.asarray(freq[None, :]), jnp.asarray(swap, jnp.bfloat16), text_count,
    )
    out, tout = pl.pallas_call(
        settle,
        name="settle",
        out_shape=(jax.ShapeDtypeStruct(out.shape, out.dtype), jax.ShapeDtypeStruct(tout.shape, tout.dtype)),
        in_specs=[vmem] * 2,
        out_specs=(vmem, vmem),
        compiler_params=pltpu.CompilerParams(vmem_limit_bytes=4 * 2**20),
    )(out, tout)
    video_out = jnp.swapaxes(out.reshape(all_heads, tokens, dim), 0, 1)
    text_out = jnp.swapaxes(tout.reshape(PAIR * heads, share, dim), 0, 1)
    return (video_out, text_out)


def solution(mesh):
    return jax.shard_map(
        functools.partial(local, mesh.shape["ctx"], mesh.shape["hd"]),
        mesh=mesh,
        in_specs=(
            P(("ctx", "hd"), "grp", None),
            P(("ctx", "hd"), "grp", None),
            P(("ctx", "hd"), "grp", None),
            P(None, ("ctx", "hd")),
            P(None, ("grp", "hd"), None),
            P(None, ("grp", "hd"), None),
            P(None, ("grp", "hd"), None),
            P(),
        ),
        out_specs=(P(("ctx", "hd"), "grp", None), P("ctx", ("grp", "hd"), None)),
        check_vma=False,
    )
```

```python
import functools
import math

import jax
import jax.numpy as jnp
import numpy as np
from jax import lax
from jax.experimental import pallas as pl
from jax.experimental.pallas import tpu as pltpu
from jax.sharding import PartitionSpec as P

THETA = 256.0
MESH = pl.DeviceIdType.MESH
PAIR = 2
NEAR = 2


def bands(dim):
    band_t = dim // 8
    band_h = (dim - band_t) // 2
    return (band_t, band_h, dim - band_t - band_h)


def constants(dim):
    freq = np.zeros((dim,), np.float32)
    swap = np.zeros((dim, dim), np.float32)
    start = 0
    for size in bands(dim):
        half = size // 2
        for i in range(half):
            low, high = start + i, start + half + i
            freq[low] = freq[high] = np.float32(THETA ** (-2.0 * i / size))
            swap[high, low] = -1.0
            swap[low, high] = 1.0
        start += size
    return freq, swap


def each(count, body):
    if count <= 4:
        for i in range(count):
            body(i)
    else:
        lax.fori_loop(0, count, lambda i, _: (body(i), 0)[1], 0)


def kernel(far, hds, q_ref, k_ref, v_ref, tq_ref, tk_ref, tv_ref, pos_in, freq_in, swap_in, count_ref,
           out_ref, tout_ref, pos_ref, freq_ref, swap_ref, qin, kin, tqs, tks, tvs, qs, ks, qg, kv, ost, tst, acc, peak, total, probs,
           in_sems, a_send, q_recv, kv_recv, f_send, n_send, o_send, o_recv, t_sems):
    ctx = lax.axis_index("ctx")
    hd = lax.axis_index("hd")
    fi, mi, ni = ctx // (PAIR * NEAR), (ctx // NEAR) % PAIR, ctx % NEAR
    groups = PAIR * hds
    heads = v_ref.shape[1]
    tokens, dim = v_ref.shape[2], v_ref.shape[3]
    mine = hd * PAIR + mi
    slot = fi * NEAR + ni

    def at(f, m, n, h):
        return {"ctx": (f * PAIR + m) * NEAR + n, "hd": h}

    def group_of(d):
        return lax.rem(hd + d // PAIR, hds) * PAIR + lax.rem(mi + d % PAIR, PAIR)

    def group_peer(d):
        g = group_of(d)
        return g, at(fi, g % PAIR, ni, g // PAIR)

    straight_first = [d for d in range(PAIR, groups, PAIR)]
    rest = [d for d in range(1, groups) if d % PAIR]
    early = [(0, 0), (1, 0)] + [(w, d) for d in straight_first for w in range(2)] + [(0, d) for d in rest]
    late = [(1, d) for d in rest]

    def far_peer(d):
        f = lax.rem(fi + d, far)
        return f, at(f, mi, ni, hd)

    def near_peer(d):
        n = lax.rem(ni + d, NEAR)
        return n, at(fi, mi, n, hd)

    text_heads = pl.ds(mi * heads, heads)
    k_in = pltpu.make_async_copy(k_ref, kin, in_sems.at[0])
    q_in = pltpu.make_async_copy(q_ref, qin, in_sems.at[1])
    v_in = pltpu.make_async_copy(v_ref.at[mine], kv.at[slot, 1, mine], in_sems.at[2])
    text_in = (
        pltpu.make_async_copy(tq_ref.at[text_heads], tqs, in_sems.at[3]),
        pltpu.make_async_copy(tk_ref.at[text_heads], tks, in_sems.at[4]),
        pltpu.make_async_copy(tv_ref.at[text_heads], tvs, in_sems.at[5]),
    )
    table_in = (
        pltpu.make_async_copy(pos_in, pos_ref, in_sems.at[6]),
        pltpu.make_async_copy(freq_in, freq_ref, in_sems.at[7]),
        pltpu.make_async_copy(swap_in, swap_ref, in_sems.at[8]),
    )
    barrier = pltpu.get_barrier_semaphore()

    def greet(peer):
        pl.semaphore_signal(barrier, inc=1, device_id=peer, device_id_type=MESH)

    each(groups - 1, lambda i: greet(group_peer(i + 1)[1]))
    each(far - 1, lambda i: greet(far_peer(i + 1)[1]))
    each(NEAR - 1, lambda i: greet(near_peer(i + 1)[1]))

    for copy in table_in + (k_in, q_in, v_in) + text_in:
        copy.start()
    for copy in table_in:
        copy.wait()
    swap = swap_ref[...]
    diagonal = (lax.broadcasted_iota(jnp.int32, (tokens, tokens), 0)
                == lax.broadcasted_iota(jnp.int32, (tokens, tokens), 1))
    lane = lax.broadcasted_iota(jnp.int32, (tokens, dim), 1)

    def column(axis):
        row = pos_ref[axis:axis + 1, :].astype(jnp.float32)
        return jnp.sum(jnp.where(diagonal, row, 0.0), axis=1, keepdims=True)

    band_t, band_h, _ = bands(dim)
    angle = jnp.where(lane < band_t, column(0), jnp.where(lane < band_t + band_h, column(1), column(2))) * freq_ref[...]
    cos, sin = jnp.cos(angle), jnp.sin(angle)

    def rotate(src, dst):
        for g in range(groups):
            for h in range(heads):
                x = src[g, h]
                turned = jnp.dot(x, swap, preferred_element_type=jnp.float32)
                dst[g, h] = (x.astype(jnp.float32) * cos + turned * sin).astype(jnp.bfloat16)

    k_in.wait()
    rotate(kin, ks)
    q_in.wait()
    rotate(qin, qs)
    kv[slot, 0, mine] = ks[mine]
    qg[mine] = qs[mine]
    v_in.wait()
    pl.semaphore_wait(barrier, (groups - 1) + (far - 1) + (NEAR - 1))

    def remote(src, dst, send, recv, peer):
        return pltpu.make_async_remote_copy(src_ref=src, dst_ref=dst, send_sem=send, recv_sem=recv,
                                            device_id=peer, device_id_type=MESH)

    def kv_to_group(w, d):
        g, peer = group_peer(d)
        src = ks if w == 0 else v_ref
        return remote(src.at[g], kv.at[slot, w, mine], a_send.at[w, d], kv_recv.at[slot, w, mine], peer)

    def q_to_group(d):
        g, peer = group_peer(d)
        return remote(qs.at[g], qg.at[mine], a_send.at[2, d], q_recv.at[mine], peer)

    def kv_to_far(w, g, d):
        f, peer = far_peer(d)
        piece = kv.at[slot, w, g]
        return remote(piece, piece, f_send.at[d, w, g], kv_recv.at[slot, w, g], peer)

    def kv_to_near(s, w, g, d):
        n, peer = near_peer(d)
        piece = kv.at[s, w, g]
        return remote(piece, piece, n_send.at[s // NEAR, w, g], kv_recv.at[s, w, g], peer)

    def arrived(s, w, g):
        piece = kv.at[s, w, g]
        remote(piece, piece, n_send.at[0, w, g], kv_recv.at[s, w, g], near_peer(1)[1]).wait_recv()

    def spread(w, g):
        each(far - 1, lambda i: kv_to_far(w, g, i + 1).start())
        kv_to_near(slot, w, g, 1).start()

    for w, d in (early + late)[2:]:
        kv_to_group(w, d).start()
    for d in straight_first + rest:
        q_to_group(d).start()
    for w in range(2):
        spread(w, mine)
    for w, d in (early + late)[2:]:
        g = group_of(d)
        arrived(slot, w, g)
        spread(w, g)

    scale = math.log2(math.e) / math.sqrt(dim)
    rows = groups * tokens

    def queries(h):
        own_text = [tqs[h, (fi * PAIR + m) * NEAR + ni] for m in range(PAIR)]
        return jnp.concatenate([qg[:, h].reshape(rows, dim)] + own_text, axis=0)

    def score(h, keys):
        return lax.dot_general(queries(h), keys, (((1,), (1,)), ((), ())), preferred_element_type=jnp.float32) * scale

    for d in range(1, groups):
        g = group_of(d)
        remote(qg.at[g], qg.at[g], a_send.at[2, d], q_recv.at[g], group_peer(d)[1]).wait_recv()
    for copy in text_in:
        copy.wait()

    def start_text():
        for h in range(heads):
            s = score(h, tks[h])
            live = lax.broadcasted_iota(jnp.int32, s.shape, 1) < count_ref[0]
            s = jnp.where(live, s, -jnp.inf)
            top = jnp.max(s, axis=1, keepdims=True)
            p = jnp.exp2(s - top)
            peak[h] = top
            total[h] = jnp.sum(p, axis=1, keepdims=True)
            acc[h] = jnp.dot(p.astype(jnp.bfloat16), tvs[h], preferred_element_type=jnp.float32)

    def keys_of(s, h):
        return kv[s, 0, :, h].reshape(rows, dim)

    def values_of(s, h):
        return kv[s, 1, :, h].reshape(rows, dim)

    def weigh(h, keys):
        sc = score(h, keys)
        old = peak[h]
        top = jnp.maximum(old, jnp.max(sc, axis=1, keepdims=True))
        p = jnp.exp2(sc - top)
        factor = jnp.exp2(old - top)
        peak[h] = top
        total[h] = total[h] * factor + jnp.sum(p, axis=1, keepdims=True)
        return p.astype(jnp.bfloat16), factor

    def absorb(s):
        for h in range(heads):
            p, factor = weigh(h, keys_of(s, h))
            acc[h] = acc[h] * factor + jnp.dot(p, values_of(s, h), preferred_element_type=jnp.float32)

    other = near_peer(1)[0]
    near_slot = fi * NEAR + other

    def from_far(i):
        f = far_peer(i + 1)[0]
        return f * NEAR + ni, f * NEAR + other

    def relay(i, w, d):
        s, g = from_far(i)[0], group_of(d)
        arrived(s, w, g)
        kv_to_near(s, w, g, 1).start()

    def take(s, w):
        for d in range(groups):
            arrived(s, w, group_of(d))

    def whole(i):
        for w, d in early + late:
            relay(i, w, d)
        straight, across = from_far(i)
        absorb(straight)
        take(across, 0)
        take(across, 1)
        absorb(across)

    start_text()
    each(far - 2, whole)
    last = far - 2
    straight, across = from_far(last)
    relay(last, 0, 0)
    relay(last, 1, 0)
    absorb(slot)
    for w, d in early[2:]:
        relay(last, w, d)
    take(near_slot, 0)
    take(near_slot, 1)
    absorb(near_slot)
    for w, d in late:
        relay(last, w, d)
    take(across, 0)
    for h in range(heads):
        p, factor = weigh(h, jnp.concatenate([keys_of(straight, h), keys_of(across, h)], axis=0))
        probs[h] = p
        acc[h] = acc[h] * factor
    for h in range(heads):
        acc[h] += jnp.dot(probs[h, :, :rows], values_of(straight, h), preferred_element_type=jnp.float32)
    take(across, 1)

    def out_to(h, d):
        g, peer = group_peer(d)
        return remote(ost.at[h, g], out_ref.at[mine, h], o_send.at[h, d], o_recv.at[h, mine], peer)

    partner = lax.rem(mi + 1, PAIR)

    def text_to(h):
        return remote(tst.at[h, partner], tout_ref.at[mi, h], t_sems.at[0, h], t_sems.at[1, h],
                      at(fi, partner, ni, hd))

    for h in range(heads):
        mixed = acc[h] + jnp.dot(probs[h, :, rows:], values_of(across, h), preferred_element_type=jnp.float32)
        result = (mixed / total[h]).astype(jnp.bfloat16)
        ost[h] = result[:rows].reshape(groups, tokens, dim)
        tst[h] = result[rows:].reshape(tst.shape[1:])
        for d in range(1, groups):
            out_to(h, d).start()
        text_to(h).start()
        out_ref[mine, h] = ost[h, mine]
        tout_ref[mi, h] = tst[h, mi]

    for d in range(1, groups):
        kv_to_group(0, d).wait_send()
        kv_to_group(1, d).wait_send()
        q_to_group(d).wait_send()
    for w in range(2):
        for d in range(groups):
            g = group_of(d)
            each(far - 1, lambda i: kv_to_far(w, g, i + 1).wait_send())
            each(far, lambda i: kv_to_near(far_peer(i)[0] * NEAR + ni, w, g, 1).wait_send())
    for h in range(heads):
        for d in range(1, groups):
            g, peer = group_peer(d)
            out_to(h, d).wait_send()
            remote(ost.at[h, g], out_ref.at[g, h], o_send.at[h, d], o_recv.at[h, g], peer).wait_recv()
        text_to(h).wait_send()
        remote(tst.at[h, partner], tout_ref.at[partner, h], t_sems.at[0, h], t_sems.at[1, h],
               at(fi, partner, ni, hd)).wait_recv()


def settle(out_ref, tout_ref, video_ref, text_ref):
    video_ref[...] = out_ref[...]
    text_ref[...] = tout_ref[...]


def local(ctxs, hds, video_q, video_k, video_v, positions, text_q, text_k, text_v, text_count):
    tokens, all_heads, dim = video_q.shape
    text = text_q.shape[0]
    groups = PAIR * hds
    heads = all_heads // groups
    far = ctxs // (PAIR * NEAR)
    share = text // ctxs
    rows = groups * tokens + PAIR * share
    freq, swap = constants(dim)

    def by_head(x):
        return jnp.swapaxes(x, 0, 1).reshape(groups, heads, tokens, dim)

    vmem = pl.BlockSpec(memory_space=pltpu.VMEM)
    dma = pltpu.SemaphoreType.DMA
    slots = far * NEAR
    out, tout = pl.pallas_call(
        functools.partial(kernel, far, hds),
        name="joint_attention",
        out_shape=(
            jax.ShapeDtypeStruct((groups, heads, tokens, dim), jnp.bfloat16),
            jax.ShapeDtypeStruct((PAIR, heads, share, dim), jnp.bfloat16),
        ),
        in_specs=[pl.BlockSpec(memory_space=pl.ANY)] * 9 + [pl.BlockSpec(memory_space=pltpu.SMEM)],
        out_specs=(vmem, vmem),
        scratch_shapes=[
            pltpu.VMEM(positions.shape, jnp.int32),
            pltpu.VMEM((1, dim), jnp.float32),
            pltpu.VMEM((dim, dim), jnp.bfloat16),
            pltpu.VMEM((groups, heads, tokens, dim), jnp.bfloat16),
            pltpu.VMEM((groups, heads, tokens, dim), jnp.bfloat16),
            pltpu.VMEM((heads, ctxs, share, dim), jnp.bfloat16),
            pltpu.VMEM((heads, text, dim), jnp.bfloat16),
            pltpu.VMEM((heads, text, dim), jnp.bfloat16),
            pltpu.VMEM((groups, heads, tokens, dim), jnp.bfloat16),
            pltpu.VMEM((groups, heads, tokens, dim), jnp.bfloat16),
            pltpu.VMEM((groups, heads, tokens, dim), jnp.bfloat16),
            pltpu.VMEM((slots, 2, groups, heads, tokens, dim), jnp.bfloat16),
            pltpu.VMEM((heads, groups, tokens, dim), jnp.bfloat16),
            pltpu.VMEM((heads, PAIR, share, dim), jnp.bfloat16),
            pltpu.VMEM((heads, rows, dim), jnp.float32),
            pltpu.VMEM((heads, rows, 1), jnp.float32),
            pltpu.VMEM((heads, rows, 1), jnp.float32),
            pltpu.VMEM((heads, rows, 2 * groups * tokens), jnp.bfloat16),
            dma((9,)),
            dma((3, groups)),
            dma((groups,)),
            dma((slots, 2, groups)),
            dma((far, 2, groups)),
            dma((far, 2, groups)),
            dma((heads, groups)),
            dma((heads, groups)),
            dma((2, heads)),
        ],
        compiler_params=pltpu.CompilerParams(
            collective_id=0, has_side_effects=True, vmem_limit_bytes=60 * 1024 * 1024
        ),
    )(
        by_head(video_q), by_head(video_k), by_head(video_v),
        jnp.swapaxes(text_q, 0, 1).reshape(PAIR * heads, ctxs, share, dim), jnp.swapaxes(text_k, 0, 1), jnp.swapaxes(text_v, 0, 1),
        positions, jnp.asarray(freq[None, :]), jnp.asarray(swap, jnp.bfloat16), text_count,
    )
    out, tout = pl.pallas_call(
        settle,
        name="settle",
        out_shape=(jax.ShapeDtypeStruct(out.shape, out.dtype), jax.ShapeDtypeStruct(tout.shape, tout.dtype)),
        in_specs=[vmem] * 2,
        out_specs=(vmem, vmem),
    )(out, tout)
    video_out = jnp.swapaxes(out.reshape(all_heads, tokens, dim), 0, 1)
    text_out = jnp.swapaxes(tout.reshape(PAIR * heads, share, dim), 0, 1)
    return (video_out, text_out)


def solution(mesh):
    return jax.shard_map(
        functools.partial(local, mesh.shape["ctx"], mesh.shape["hd"]),
        mesh=mesh,
        in_specs=(
            P(("ctx", "hd"), "grp", None),
            P(("ctx", "hd"), "grp", None),
            P(("ctx", "hd"), "grp", None),
            P(None, ("ctx", "hd")),
            P(None, ("grp", "hd"), None),
            P(None, ("grp", "hd"), None),
            P(None, ("grp", "hd"), None),
            P(),
        ),
        out_specs=(P(("ctx", "hd"), "grp", None), P("ctx", ("grp", "hd"), None)),
        check_vma=False,
    )
```
